128 devices in a mesh: tm: 4 (over x_lo, core), space: 32 (over x_hi, y, z).
Axes of the slice: x: 4 (x_hi: 2, x_lo: 2; x = x_hi * 2 + x_lo), y: 4, z: 4, core: 2. Of those that a mesh axis runs over, the one named last changes fastest.
Arguments:
- forcing: bfloat16 [4, 4, 6, 256, 4096], P('tm', None, None, None, 'space'), may hold values from -6 to 6
- zonal_courant: float32 [4, 256, 4096], P('tm', None, 'space'), may hold values from -0.3 to 0.3
- meridional_courant: float32 [4, 256, 4096], P('tm', None, 'space'), may hold values from -0.3 to 0.3
- zonal_faces: float32 [4, 256, 4096], P('tm', None, 'space'), may hold values from 0.1 to 0.4
- meridional_faces: float32 [4, 256, 4096], P('tm', None, 'space'), may hold values from 0.1 to 0.4
- coupling: float32 [4, 6, 6], P('tm'), may hold values from -0.375 to 0.375
Outputs:
- adjoint_start: float32 [4, 6, 256, 4096], P('tm', None, None, 'space')
The draws below stay inside these ranges and needn't reach their ends.
All inputs are finite; a program needn't handle non-finite values.
Results may differ from the reference program's by a relative error of at most 0.0015.
Values may be sent and summed in bfloat16 or wider, within the bound.
A program may use at most 64 MiB of HBM per device.

```python
import math
import jax
import jax.numpy as jnp
from jax import lax

F = 6
NLAT = 256
STEPS = 4
SWEEPS = 2
NSUB = 4
NLON = 4096


def steps_of(stream_key, dims, pieces, least, high):
    loudness = 1.0
    for position, parts in pieces:
        draws = jax.random.uniform(jax.random.fold_in(jax.random.fold_in(stream_key, 6), position), (parts,), jnp.float32, least / len(pieces), high / len(pieces))
        loudness = loudness * jnp.repeat(jnp.exp(draws), dims[position] // parts).reshape((-1,) + (1,) * (len(dims) - 1 - position))
    return loudness


def scatter_about(rng, extent, deviation, bound, cuts=(), kind=jnp.bfloat16):
    array = jax.random.normal(rng, extent, jnp.float32) * deviation
    if len(cuts) > 0:
        array = steps_of(rng, extent, cuts, -0.22, 0.18) * array
    return jnp.clip(array, min=-bound, max=bound).astype(kind)


def setup_inputs(seed: int = 0) -> dict:
    key_of = jax.random.split(jax.random.key(seed), 7)
    return {
        "forcing": scatter_about(key_of[0], (NSUB, STEPS, F, NLAT, NLON), 1.0, 6.0, ((0, 4), (4, 32))),
        "zonal_courant": jnp.clip(jax.random.uniform(key_of[1], (NSUB, NLAT, NLON), jnp.float32, -0.3, 0.3) * steps_of(key_of[1], (NSUB, NLAT, NLON), ((0, 4), (2, 32)), -0.4, 0.0), -0.3, 0.3),
        "meridional_courant": jnp.clip(jax.random.uniform(key_of[2], (NSUB, NLAT, NLON), jnp.float32, -0.3, 0.3) * steps_of(key_of[2], (NSUB, NLAT, NLON), ((0, 4), (2, 32)), -0.4, 0.0), -0.3, 0.3),
        "zonal_faces": jnp.clip(jnp.exp(math.log(0.4) - 1.3862944 * jax.random.uniform(key_of[3], (NSUB, NLAT, NLON), jnp.float32) ** steps_of(key_of[3], (NSUB, NLAT, NLON), ((0, 4), (2, 32)), -0.2, 0.2)), 0.1, 0.4),
        "meridional_faces": jnp.clip(jnp.exp(math.log(0.4) - 1.3862944 * jax.random.uniform(key_of[4], (NSUB, NLAT, NLON), jnp.float32) ** steps_of(key_of[4], (NSUB, NLAT, NLON), ((0, 4), (2, 32)), -0.2, 0.2)), 0.1, 0.4),
        "coupling": scatter_about(key_of[5], (NSUB, F, F), 0.06, 0.375, ((0, 4),), jnp.float32),
    }


OMEGA = 0.4


def north(values):
    zero_edge = jnp.zeros_like(values[..., :1, :])
    return jnp.concatenate([values[..., 1:, :], zero_edge], axis=-2)


def south(values):
    zero_edge = jnp.zeros_like(values[..., :1, :])
    return jnp.concatenate([zero_edge, values[..., :-1, :]], axis=-2)


def operator_h(state_now, face_east, northern):
    face_west = jnp.roll(face_east, 1, axis=-1)
    east_side = jnp.roll(state_now, -1, axis=-1)
    west_side = jnp.roll(state_now, 1, axis=-1)
    return (state_now + face_east * (state_now - east_side) + face_west * (state_now - west_side)
            + northern * (state_now - north(state_now)) + south(northern) * (state_now - south(state_now)))


def smoother(source, face_east, northern):
    smoothed = OMEGA * source
    for sweep_index in range(SWEEPS):
        smoothed = smoothed + OMEGA * (source - operator_h(smoothed, face_east, northern))
    return smoothed


def transposed_explicit(smoothed, courant_x, courant_y, coupling_now):
    zonal_flux = courant_x * smoothed
    meridional_flux = courant_y * smoothed
    mixing = jnp.einsum("gf,gab->fab", coupling_now, smoothed, precision=lax.Precision.HIGHEST)
    zonal_term = 0.5 * (jnp.roll(zonal_flux, -1, axis=-1) - jnp.roll(zonal_flux, 1, axis=-1))
    meridional_term = 0.5 * (north(meridional_flux) - south(meridional_flux))
    return smoothed + mixing + zonal_term + meridional_term


def reference(forcing, zonal_courant, meridional_courant, zonal_faces, meridional_faces, coupling):
    row_index = lax.broadcasted_iota(jnp.int32, meridional_faces.shape, 1)
    northern_all = jnp.where(row_index < NLAT - 1, meridional_faces, jnp.zeros_like(meridional_faces))
    adjoint = jnp.zeros((F, NLAT, NLON), jnp.float32)
    starts = []
    for window in reversed(range(NSUB)):
        for step_index in reversed(range(STEPS)):
            smoothed = smoother(adjoint, zonal_faces[window], northern_all[window])
            adjoint = transposed_explicit(smoothed, zonal_courant[window], meridional_courant[window], coupling[window])
            adjoint = adjoint + forcing[window, step_index].astype(jnp.float32)
        starts.append(adjoint)
    return jnp.stack(starts[::-1], axis=0)
```

```python
import functools

import jax
import jax.numpy as jnp
from jax import lax
from jax.experimental import pallas as pl
from jax.experimental.pallas import tpu as pltpu
from jax.sharding import PartitionSpec as P

OMEGA = 0.4
STEPS = 4
F = 6
HALO = 16
HALF = 64
FRAME = HALF + 2 * HALO
T = 11
BASE = (FRAME - 8 * T) // 2
EXT = {3: 16, 2: 8, 1: 8, 0: 0}
MESH = pl.DeviceIdType.MESH


def strided(t):
    return pl.ds(BASE + t, 8, stride=T)


def body(
    forcing, courant_x, courant_y, faces_x, faces_y, coupling, out,
    nat_f, nat_o, even_odd, tr_f, tr_o, fr, op, cp,
    co, mix, r, x1, x2, adj, edge_out, edge_in, hand_out, hand_in, res, outv,
    load_sem, out_sem, loc_sem, part_send, part_recv, ext_send, ext_recv,
    edge_send, edge_recv, hand_send, hand_recv, res_sem,
):
    tm = lax.axis_index("tm")
    space = lax.axis_index("space")
    n_space = lax.axis_size("space")
    h = lax.rem(tm, 2)
    o = 1 - h
    pair = tm // 2

    def at_space(d):
        return lax.rem(space + d + n_space, n_space)

    partner = (2 * pair + o, space)
    to_east = (2 * pair, at_space(1))
    to_west = (2 * pair + 1, at_space(-1))

    ops_in = (faces_x, faces_y, courant_x, courant_y)
    loads = [pltpu.make_async_copy(ops_in[i].at[0], nat_o.at[i], load_sem.at[i]) for i in range(4)]
    loads.append(pltpu.make_async_copy(coupling.at[0], cp.at[h], load_sem.at[4]))
    loads += [pltpu.make_async_copy(forcing.at[0, k], nat_f.at[k], load_sem.at[5 + k]) for k in range(STEPS)]
    for i in (0, 1, 2, 3, 4, 8, 7, 6, 5):
        loads[i].start()

    barrier = pltpu.get_barrier_semaphore()
    count = 0
    for d in (-1, 0, 1):
        for j in range(4):
            if d == 0 and j == 0:
                continue
            other = lax.rem(tm + j, 4)
            pl.semaphore_signal(barrier, inc=1, device_id=(other, at_space(d)), device_id_type=MESH)
            count += 1

    def views(c):
        if c == STEPS:
            return tr_o, (lambda slot: op.at[slot]), HALO
        return tr_f.at[c], (lambda slot: fr.at[slot, c]), EXT[c]

    def own_copy(c):
        src, dst, _ = views(c)
        return pltpu.make_async_copy(
            src.at[:, :, pl.ds(pl.multiple_of(48 * h, 16), 80)],
            dst(h).at[:, :, pl.ds(pl.multiple_of(16 * o, 16), 80)],
            loc_sem.at[c],
        )

    def partner_copy(c):
        src, dst, _ = views(c)
        return pltpu.make_async_remote_copy(
            src_ref=src.at[:, :, pl.ds(pl.multiple_of(48 * o, 16), 80)],
            dst_ref=dst(h).at[:, :, pl.ds(pl.multiple_of(16 * h, 16), 80)],
            send_sem=part_send.at[c], recv_sem=part_recv.at[c],
            device_id=partner, device_id_type=MESH,
        )

    def partner_arrival(c):
        src, dst, _ = views(c)
        return pltpu.make_async_remote_copy(
            src_ref=src.at[:, :, pl.ds(pl.multiple_of(48 * h, 16), 80)],
            dst_ref=dst(o).at[:, :, pl.ds(pl.multiple_of(16 * o, 16), 80)],
            send_sem=part_send.at[c], recv_sem=part_recv.at[c],
            device_id=partner, device_id_type=MESH,
        )

    def ext_copies(c):
        src, dst, n = views(c)
        if n == 0:
            return []
        east = pltpu.make_async_remote_copy(
            src_ref=src.at[:, :, pl.ds(128 - n, n)],
            dst_ref=dst(h).at[:, :, pl.ds(HALO - n, n)],
            send_sem=ext_send.at[0, c], recv_sem=ext_recv.at[h, c],
            device_id=to_east, device_id_type=MESH,
        )
        west = pltpu.make_async_remote_copy(
            src_ref=src.at[:, :, pl.ds(0, n)],
            dst_ref=dst(h).at[:, :, pl.ds(HALO + HALF, n)],
            send_sem=ext_send.at[1, c], recv_sem=ext_recv.at[h, c],
            device_id=to_west, device_id_type=MESH,
        )
        return [east, west]

    def ext_arrival(slot, c):
        src, dst, n = views(c)
        start = pl.multiple_of((HALO - n) * o + (HALO + HALF) * h, 8)
        return pltpu.make_async_remote_copy(
            src_ref=src.at[:, :, pl.ds(0, n)],
            dst_ref=dst(slot).at[:, :, pl.ds(start, n)],
            send_sem=ext_send.at[0, c], recv_sem=ext_recv.at[slot, c],
            device_id=to_east, device_id_type=MESH,
        )

    def send_chunk(c):
        own_copy(c).start()
        partner_copy(c).start()
        for copy in ext_copies(c):
            copy.start()

    def wait_chunk(slot, c):
        @pl.when(h == slot)
        def _():
            own_copy(c).wait()

        @pl.when(h != slot)
        def _():
            partner_arrival(c).wait_recv()

        if views(c)[2]:
            ext_arrival(slot, c).wait_recv()

    cp_copy = pltpu.make_async_remote_copy(
        src_ref=cp.at[h], dst_ref=cp.at[h],
        send_sem=part_send.at[5], recv_sem=part_recv.at[5],
        device_id=partner, device_id_type=MESH,
    )

    cp_arrival = pltpu.make_async_remote_copy(
        src_ref=cp.at[o], dst_ref=cp.at[o],
        send_sem=part_send.at[5], recv_sem=part_recv.at[5],
        device_id=partner, device_id_type=MESH,
    )

    zero8 = jnp.zeros((F, 2, 8, 128), jnp.float32)
    for slot in range(2):
        for c in (1, 2):
            fr[slot, c, :, :, pl.ds(pl.multiple_of((FRAME - 8) * h, 8), 8)] = zero8
        start = pl.multiple_of(80 * h, 16)
        fr[slot, 0, :, :, pl.ds(start, 16)] = jnp.zeros((F, 2, 16, 128), jnp.float32)

    for i in range(5):
        loads[i].wait()
    for i in range(4):
        for p in range(2):
            tr_o[i, p] = jnp.transpose(nat_o[i, pl.ds(p, 128, stride=2), :])
    pl.semaphore_wait(barrier, count)
    cp_copy.start()
    send_chunk(STEPS)
    for k in (3, 2, 1, 0):
        loads[5 + k].wait()

        def one(f, carry, k=k):
            even_odd[...] = OMEGA * nat_f[k, f].astype(jnp.float32)
            for p in range(2):
                tr_f[k, f, p] = jnp.transpose(even_odd[pl.ds(p, 128, stride=2), :])
            return carry

        lax.fori_loop(0, F, one, 0)
        send_chunk(k)

    lane = lax.broadcasted_iota(jnp.int32, (8, 128), 1)

    def coefficients(slot):
        @pl.when(h == slot)
        def _():
            cp_copy.wait_send()

        @pl.when(h != slot)
        def _():
            cp_arrival.wait_recv()

        table = cp[slot]
        for g in range(F):
            for f in range(F):
                value = jnp.broadcast_to(table[g:g + 1, f:f + 1], (8, 128))
                mix[g, f] = OMEGA * (value + 1.0) if g == f else OMEGA * value

        def one(t, carry):
            def get(i, p, d=0):
                return op[slot, i, p, pl.ds(BASE + t + d, 8, stride=T), :]

            b0, b1 = OMEGA * get(1, 0), OMEGA * get(1, 1)
            v0, v1 = 0.5 * OMEGA * get(3, 0), 0.5 * OMEGA * get(3, 1)
            north = (b0, jnp.where(lane == 127, 0.0, b1))
            south = (jnp.where(lane == 0, 0.0, pltpu.roll(b1, 1, 1)), b0)
            v_north = (v1, jnp.where(lane == 127, 0.0, pltpu.roll(v0, 127, 1)))
            v_south = (jnp.where(lane == 0, 0.0, -pltpu.roll(v1, 1, 1)), -v0)
            for p in range(2):
                east, west = OMEGA * get(0, p), OMEGA * get(0, p, -1)
                co[t, p, 0] = (1.0 - OMEGA) - (east + west + north[p] + south[p])
                co[t, p, 1] = east
                co[t, p, 2] = west
                co[t, p, 3] = north[p]
                co[t, p, 4] = south[p]
                co[t, p, 5] = 0.5 * OMEGA * get(2, p, 1)
                co[t, p, 6] = -0.5 * OMEGA * get(2, p, -1)
                co[t, p, 7] = v_north[p]
                co[t, p, 8] = v_south[p]
            return carry

        lax.fori_loop(0, T, one, 0)

    def pads(buf):
        for p in range(2):
            buf[0, p] = pltpu.roll(buf[T, p], 1, 1)
            buf[T + 1, p] = pltpu.roll(buf[1, p], 7, 1)

    def meridional(here):
        return (here[1], pltpu.roll(here[1], 1, 2)), (pltpu.roll(here[0], 127, 2), here[0])

    def sweep(src, dst, add):
        def one(t, carry):
            here = (src[t + 1, 0], src[t + 1, 1])
            beside = meridional(here)
            for p in range(2):
                diag = co[t, p, 0]
                if add is None:
                    value = (diag + 1.0) * here[p]
                else:
                    value = diag * here[p] + add[t + 1, p]
                value = value + co[t, p, 1] * src[t + 2, p] + co[t, p, 2] * src[t, p]
                value = value + co[t, p, 3] * beside[p][0] + co[t, p, 4] * beside[p][1]
                dst[t + 1, p] = value
            return carry

        lax.fori_loop(0, T, one, 0, unroll=True)
        pads(dst)

    def explicit(slot, k):
        def one(t, carry):
            here = (x2[t + 1, 0], x2[t + 1, 1])
            beside = meridional(here)
            for p in range(2):
                value = fr[slot, k, :, p, strided(t), :]
                value = value + co[t, p, 5] * x2[t + 2, p] + co[t, p, 6] * x2[t, p]
                value = value + co[t, p, 7] * beside[p][0] + co[t, p, 8] * beside[p][1]
                for g in range(F):
                    value = value + mix[g] * here[p][g]
                r[t + 1, p] = value
            return carry

        lax.fori_loop(0, T, one, 0, unroll=True)
        pads(r)

    def wait_forcing(slot, k):
        for c in range(STEPS):
            @pl.when(k == c)
            def _(c=c):
                wait_chunk(slot, c)

    def steps(slot, first):
        def one(n, carry):
            k = STEPS - 1 - n
            sweep(r, x1, None)
            sweep(x1, x2, r)
            wait_forcing(slot, k)
            explicit(slot, k)
            return carry

        lax.fori_loop(first, STEPS, one, 0)

    def from_frame(ref):
        for t in range(T):
            for p in range(2):
                r[t + 1, p] = ref[:, p, strided(t), :]
        pads(r)

    def to_frame(ref):
        for t in range(T):
            for p in range(2):
                ref[:, p, strided(t), :] = r[t + 1, p]

    def edge_copies(target_pair, out_ref, in_ref, send, recv):
        west = (2 * target_pair + o, at_space(-o))
        east = (2 * target_pair + o, at_space(h))
        return [
            pltpu.make_async_remote_copy(
                src_ref=out_ref.at[:, :, pl.ds(HALO, HALO)],
                dst_ref=in_ref.at[:, :, pl.ds(HALO + HALF, HALO)],
                send_sem=send.at[0], recv_sem=recv.at[1],
                device_id=west, device_id_type=MESH,
            ),
            pltpu.make_async_remote_copy(
                src_ref=out_ref.at[:, :, pl.ds(HALF, HALO)],
                dst_ref=in_ref.at[:, :, pl.ds(0, HALO)],
                send_sem=send.at[1], recv_sem=recv.at[0],
                device_id=east, device_id_type=MESH,
            ),
        ]

    def hand_main():
        return pltpu.make_async_remote_copy(
            src_ref=hand_out.at[:, :, pl.ds(HALO, HALF)],
            dst_ref=hand_in.at[:, :, pl.ds(HALO, HALF)],
            send_sem=hand_send.at[2], recv_sem=hand_recv.at[2],
            device_id=(h, space), device_id_type=MESH,
        )

    def result_copy(phase):
        return pltpu.make_async_remote_copy(
            src_ref=adj.at[phase, :, :, pl.ds(HALO, HALF)],
            dst_ref=res.at[:, :, pl.ds(pl.multiple_of(HALF * h, HALF), HALF)],
            send_sem=res_sem.at[0], recv_sem=res_sem.at[1],
            device_id=partner, device_id_type=MESH,
        )

    result_arrival = pltpu.make_async_remote_copy(
        src_ref=adj.at[0, :, :, pl.ds(HALO, HALF)],
        dst_ref=res.at[:, :, pl.ds(pl.multiple_of(HALF * o, HALF), HALF)],
        send_sem=res_sem.at[0], recv_sem=res_sem.at[1],
        device_id=partner, device_id_type=MESH,
    )

    first = pair
    wait_chunk(1, STEPS)
    coefficients(1)

    @pl.when(pair == 1)
    def _():
        wait_chunk(1, 3)
        from_frame(fr.at[1, 3])

    @pl.when(pair == 0)
    def _():
        hand_main().wait_recv()
        for copy in edge_copies(0, hand_out, hand_in, hand_send, hand_recv):
            copy.wait_recv()
        adj[0] = hand_in[...].astype(jnp.float32)
        from_frame(adj.at[0])

    steps(1, first)
    to_frame(adj.at[0])
    edge_out[:, :, HALO:2 * HALO] = adj[0, :, :, HALO:2 * HALO].astype(jnp.bfloat16)
    edge_out[:, :, HALF:HALF + HALO] = adj[0, :, :, HALF:HALF + HALO].astype(jnp.bfloat16)
    edges = edge_copies(pair, edge_out, edge_in, edge_send, edge_recv)
    for copy in edges:
        copy.start()

    @pl.when(h == 0)
    def _():
        result_copy(0).start()

    wait_chunk(0, STEPS)
    coefficients(0)
    for copy in edges:
        copy.wait_recv()
    adj[0, :, :, 0:HALO] = edge_in[:, :, 0:HALO].astype(jnp.float32)
    adj[0, :, :, HALO + HALF:FRAME] = edge_in[:, :, HALO + HALF:FRAME].astype(jnp.float32)
    from_frame(adj.at[0])
    steps(0, 0)
    to_frame(adj.at[1])

    @pl.when(pair == 1)
    def _():
        hand_out[:, :, HALO:HALO + HALF] = adj[1, :, :, HALO:HALO + HALF].astype(jnp.bfloat16)
        hand_main().start()
        for copy in edge_copies(0, hand_out, hand_in, hand_send, hand_recv):
            copy.start()

    @pl.when(h == 1)
    def _():
        result_copy(1).start()

    own = adj.at[1 - h]
    res[:, :, pl.ds(pl.multiple_of(HALF * h, HALF), HALF)] = own[:, :, HALO:HALO + HALF]
    result_arrival.wait_recv()

    def out_copy(f):
        return pltpu.make_async_copy(outv.at[f], out.at[0, f], out_sem.at[f])

    def finish(f, carry):
        for p in range(2):
            outv[f, pl.ds(p, 128, stride=2), :] = (1.0 / OMEGA) * jnp.transpose(res[f, p])
        out_copy(f).start()
        return carry

    lax.fori_loop(0, F, finish, 0)

    for c in range(STEPS + 1):
        partner_copy(c).wait_send()
        for copy in ext_copies(c):
            copy.wait_send()

    for copy in edges:
        copy.wait_send()
    result_copy(0).wait_send()

    @pl.when(pair == 1)
    def _():
        hand_main().wait_send()
        for copy in edge_copies(0, hand_out, hand_in, hand_send, hand_recv):
            copy.wait_send()

    for f in range(F):
        out_copy(f).wait()


def per_device(forcing, zonal_courant, meridional_courant, zonal_faces, meridional_faces, coupling):
    f32, bf16 = jnp.float32, jnp.bfloat16
    dma = pltpu.SemaphoreType.DMA
    return pl.pallas_call(
        body,
        out_shape=jax.ShapeDtypeStruct((1,) + forcing.shape[2:], f32),
        in_specs=[pl.BlockSpec(memory_space=pl.ANY)] * 6,
        out_specs=pl.BlockSpec(memory_space=pl.ANY),
        scratch_shapes=[
            pltpu.VMEM((STEPS, F, 256, 128), bf16),
            pltpu.VMEM((4, 256, 128), f32),
            pltpu.VMEM((256, 128), f32),
            pltpu.VMEM((STEPS, F, 2, 128, 128), f32),
            pltpu.VMEM((4, 2, 128, 128), f32),
            pltpu.VMEM((2, STEPS, F, 2, FRAME, 128), f32),
            pltpu.VMEM((2, 4, 2, FRAME, 128), f32),
            pltpu.VMEM((2, F, F), f32),
            pltpu.VMEM((T, 2, 9, 8, 128), f32),
            pltpu.VMEM((F, F, 8, 128), f32),
            pltpu.VMEM((T + 2, 2, F, 8, 128), f32),
            pltpu.VMEM((T + 2, 2, F, 8, 128), f32),
            pltpu.VMEM((T + 2, 2, F, 8, 128), f32),
            pltpu.VMEM((2, F, 2, FRAME, 128), f32),
            pltpu.VMEM((F, 2, FRAME, 128), bf16),
            pltpu.VMEM((F, 2, FRAME, 128), bf16),
            pltpu.VMEM((F, 2, FRAME, 128), bf16),
            pltpu.VMEM((F, 2, FRAME, 128), bf16),
            pltpu.VMEM((F, 2, 128, 128), f32),
            pltpu.VMEM((F, 256, 128), f32),
            dma((9,)),
            dma((F,)),
            dma((5,)),
            dma((6,)),
            dma((6,)),
            dma((2, 5)),
            dma((2, 5)),
            dma((2,)),
            dma((2,)),
            dma((3,)),
            dma((3,)),
            dma((2,)),
        ],
        compiler_params=pltpu.CompilerParams(
            collective_id=0, has_side_effects=True, vmem_limit_bytes=60 * 1024 * 1024
        ),
        name="adjoint_window",
    )(forcing, zonal_courant, meridional_courant, zonal_faces, meridional_faces, coupling)


def solution(mesh):
    return jax.shard_map(
        per_device,
        mesh=mesh,
        in_specs=(
            P("tm", None, None, None, "space"),
            P("tm", None, "space"),
            P("tm", None, "space"),
            P("tm", None, "space"),
            P("tm", None, "space"),
            P("tm", None, None),
        ),
        out_specs=P("tm", None, None, "space"),
        check_vma=False,
    )
```

```python
import jax
import jax.numpy as jnp
from jax import lax
from jax.experimental import pallas as pl
from jax.experimental.pallas import tpu as pltpu
from jax.sharding import PartitionSpec as P

OMEGA = 0.4
STEPS = 4
F = 6
WIDTH = 128
HALF = 64
HALO = 24
SIDE = 32
FRAME = HALF + 2 * HALO
T = FRAME // 8
ROWS = WIDTH + 2 * HALO
OPS = STEPS
EXT = ((0, 8, 8, 16, 16), (16, 16, 24, 24, 24))
MESH = pl.DeviceIdType.MESH
UNROLL = True


def body(
    forcing, courant_x, courant_y, faces_x, faces_y, coupling, out,
    nat_f, nat_o, even_odd, fr, op, cp, ops,
    co, mix, r, x1, x2, adj, hand_out, hand_in, side_in, relay_in, res, outv,
    load_sem, out_sem, part_send, part_recv, ext_send, ext_recv,
    hand_send, hand_recv, res_send, res_recv,
):
    tm = lax.axis_index("tm")
    space = lax.axis_index("space")
    n_space = lax.axis_size("space")
    h = lax.rem(tm, 2)
    o = 1 - h
    pair = tm // 2

    def at_space(d):
        return lax.rem(space + d + n_space, n_space)

    barrier = pltpu.get_barrier_semaphore()
    count = 0
    for d in (-1, 1, 0):
        for j in range(4):
            if d == 0 and j == 0:
                continue
            other = lax.rem(tm + j, 4)
            pl.semaphore_signal(barrier, inc=1, device_id=(other, at_space(d)), device_id_type=MESH)
            count += 1

    ops_in = (faces_x, faces_y, courant_x, courant_y)
    loads = [pltpu.make_async_copy(ops_in[i].at[0], nat_o.at[i], load_sem.at[i]) for i in range(4)]
    loads.append(pltpu.make_async_copy(coupling, cp.at[h], load_sem.at[4]))
    loads += [pltpu.make_async_copy(forcing.at[0, k], nat_f.at[k], load_sem.at[5 + k]) for k in range(STEPS)]
    for i in (0, 1, 2, 3, 8, 4, 7, 6, 5):
        loads[i].start()

    partner = (2 * pair + o, space)
    to_east = (2 * pair, at_space(1))
    to_west = (2 * pair + 1, at_space(-1))

    def chunk(slot, c):
        return op.at[slot] if c == OPS else fr.at[slot, c]

    def partner_copy(c):
        ref = chunk(h, c).at[:, :, pl.ds(pl.multiple_of(HALO + 40 * o, 8), 88)]
        return pltpu.make_async_remote_copy(
            src_ref=ref, dst_ref=ref, send_sem=part_send.at[c], recv_sem=part_recv.at[c],
            device_id=partner, device_id_type=MESH,
        )

    def partner_arrival(c):
        ref = chunk(o, c).at[:, :, pl.ds(pl.multiple_of(HALO + 40 * h, 8), 88)]
        return pltpu.make_async_remote_copy(
            src_ref=ref, dst_ref=ref, send_sem=part_send.at[c], recv_sem=part_recv.at[c],
            device_id=partner, device_id_type=MESH,
        )

    def ext_copies(slot, c):
        n = EXT[slot][c]
        if n == 0:
            return []
        ref = chunk(slot, c)
        east = pltpu.make_async_remote_copy(
            src_ref=ref.at[:, :, pl.ds(HALO + WIDTH - n, n)],
            dst_ref=ref.at[:, :, pl.ds(HALO - n, n)],
            send_sem=ext_send.at[0, c], recv_sem=ext_recv.at[slot, c],
            device_id=to_east, device_id_type=MESH,
        )
        west = pltpu.make_async_remote_copy(
            src_ref=ref.at[:, :, pl.ds(HALO, n)],
            dst_ref=ref.at[:, :, pl.ds(HALO + WIDTH, n)],
            send_sem=ext_send.at[1, c], recv_sem=ext_recv.at[slot, c],
            device_id=to_west, device_id_type=MESH,
        )
        return [east, west]

    def ext_arrival(slot, c):
        n = EXT[slot][c]
        start = pl.multiple_of((HALO - n) * o + (HALO + WIDTH) * h, 8)
        ref = chunk(slot, c).at[:, :, pl.ds(start, n)]
        return pltpu.make_async_remote_copy(
            src_ref=ref, dst_ref=ref, send_sem=ext_send.at[0, c], recv_sem=ext_recv.at[slot, c],
            device_id=to_east, device_id_type=MESH,
        )

    def wait_chunk(slot, c):
        @pl.when(h != slot)
        def _():
            partner_arrival(c).wait_recv()

        if EXT[slot][c]:
            ext_arrival(slot, c).wait_recv()

    def cp_copy(slot):
        return pltpu.make_async_remote_copy(
            src_ref=cp.at[slot], dst_ref=cp.at[slot],
            send_sem=part_send.at[5], recv_sem=part_recv.at[5],
            device_id=partner, device_id_type=MESH,
        )

    for slot in range(2):
        for c in range(STEPS + 1):
            n = EXT[slot][c]
            if n < HALO:
                ref = chunk(slot, c)
                start = pl.multiple_of((HALO + WIDTH + n) * h, 8)
                ref[:, :, pl.ds(start, HALO - n)] = jnp.zeros(ref.shape[:2] + (HALO - n, 128), jnp.float32)

    for i in range(4):
        loads[i].wait()
    for i in range(4):
        for p in range(2):
            op[h, i, p, HALO:HALO + WIDTH] = jnp.transpose(nat_o[i, pl.ds(p, 128, stride=2), :])
    pl.semaphore_wait(barrier, count)

    def send_first(c):
        @pl.when(h == 1)
        def _():
            for copy in ext_copies(1, c):
                copy.start()

        partner_copy(c).start()

    send_first(OPS)
    for k in (3, 2, 1, 0):
        loads[5 + k].wait()

        def one(f, carry, k=k):
            even_odd[...] = OMEGA * nat_f[k, f].astype(jnp.float32)
            for p in range(2):
                fr[h, k, f, p, HALO:HALO + WIDTH] = jnp.transpose(even_odd[pl.ds(p, 128, stride=2), :])
            return carry

        lax.fori_loop(0, F, one, 0)
        send_first(k)
        if k == 3:
            loads[4].wait()
            cp_copy(h).start()

    @pl.when(h == 0)
    def _():
        for c in (OPS, 3, 2, 1, 0):
            for copy in ext_copies(0, c):
                copy.start()

    lane = lax.broadcasted_iota(jnp.int32, (8, 128), 1)

    def frame(t):
        return pl.ds(HALF * h + t, 8, stride=T)

    def coefficients(slot):
        @pl.when(h != slot)
        def _():
            cp_copy(o).wait_recv()

        for g in range(F):
            row = cp[slot, g]
            for f in range(F):
                value = jnp.broadcast_to(row[:, f:f + 1], (8, 128))
                mix[g, f] = OMEGA * (value + 1.0) if g == f else OMEGA * value

        for i in (0, 2):
            for p in range(2):
                for t in range(T):
                    ops[i // 2, t + 1, p] = op[slot, i, p, frame(t), :]
                ops[i // 2, 0, p] = pltpu.roll(ops[i // 2, T, p], 1, 0)
                ops[i // 2, T + 1, p] = pltpu.roll(ops[i // 2, 1, p], 7, 0)

        def one(t, carry):
            def get(i, p):
                return op[slot, i, p, frame(t), :]

            b0, b1 = OMEGA * get(1, 0), OMEGA * get(1, 1)
            v0, v1 = 0.5 * OMEGA * get(3, 0), 0.5 * OMEGA * get(3, 1)
            north = (b0, jnp.where(lane == 127, 0.0, b1))
            south = (jnp.where(lane == 0, 0.0, pltpu.roll(b1, 1, 1)), b0)
            v_north = (v1, jnp.where(lane == 127, 0.0, pltpu.roll(v0, 127, 1)))
            v_south = (jnp.where(lane == 0, 0.0, -pltpu.roll(v1, 1, 1)), -v0)
            for p in range(2):
                east, west = OMEGA * ops[0, t + 1, p], OMEGA * ops[0, t, p]
                co[t, p, 0] = (1.0 - OMEGA) - (east + west + north[p] + south[p])
                co[t, p, 1] = east
                co[t, p, 2] = west
                co[t, p, 3] = north[p]
                co[t, p, 4] = south[p]
                co[t, p, 5] = 0.5 * OMEGA * ops[1, t + 2, p]
                co[t, p, 6] = -0.5 * OMEGA * ops[1, t, p]
                co[t, p, 7] = v_north[p]
                co[t, p, 8] = v_south[p]
            return carry

        lax.fori_loop(0, T, one, 0)

    def pads(buf):
        for p in range(2):
            buf[0, p] = pltpu.roll(buf[T, p], 1, 1)
            buf[T + 1, p] = pltpu.roll(buf[1, p], 7, 1)

    def meridional(here):
        return (here[1], pltpu.roll(here[1], 1, 2)), (pltpu.roll(here[0], 127, 2), here[0])

    def sweep(src, dst, add):
        def one(t, carry):
            here = (src[t + 1, 0], src[t + 1, 1])
            beside = meridional(here)
            for p in range(2):
                diag = co[t, p, 0]
                if add is None:
                    value = (diag + 1.0) * here[p]
                else:
                    value = diag * here[p] + add[t + 1, p]
                value = value + co[t, p, 1] * src[t + 2, p] + co[t, p, 2] * src[t, p]
                value = value + co[t, p, 3] * beside[p][0] + co[t, p, 4] * beside[p][1]
                dst[t + 1, p] = value
            return carry

        lax.fori_loop(0, T, one, 0, unroll=UNROLL)
        pads(dst)

    def explicit(slot, k):
        def one(t, carry):
            here = (x2[t + 1, 0], x2[t + 1, 1])
            beside = meridional(here)
            for p in range(2):
                value = fr[slot, k, :, p, frame(t), :]
                value = value + co[t, p, 5] * x2[t + 2, p] + co[t, p, 6] * x2[t, p]
                value = value + co[t, p, 7] * beside[p][0] + co[t, p, 8] * beside[p][1]
                for g in range(F):
                    value = value + mix[g] * here[p][g]
                r[t + 1, p] = value
            return carry

        lax.fori_loop(0, T, one, 0, unroll=UNROLL)
        pads(r)

    def steps(slot, first):
        def one(n, carry):
            k = STEPS - 1 - n
            sweep(r, x1, None)
            sweep(x1, x2, r)
            for c in range(STEPS):
                @pl.when(k == c)
                def _(c=c):
                    wait_chunk(slot, c)

            explicit(slot, k)
            return carry

        lax.fori_loop(first, STEPS, one, 0)

    def adj_frame(t):
        return pl.ds(SIDE - HALO + t, 8, stride=T)

    def to_adj(phase):
        for t in range(T):
            for p in range(2):
                adj[phase, :, p, adj_frame(t), :] = r[t + 1, p]

    def result_copy(phase, f):
        return pltpu.make_async_remote_copy(
            src_ref=adj.at[phase, f, :, pl.ds(SIDE, HALF)],
            dst_ref=res.at[f, :, pl.ds(pl.multiple_of(HALF * h, HALF), HALF)],
            send_sem=res_send.at[f], recv_sem=res_recv.at[f],
            device_id=partner, device_id_type=MESH,
        )

    def result_arrival(f):
        return pltpu.make_async_remote_copy(
            src_ref=adj.at[0, f, :, pl.ds(SIDE, HALF)],
            dst_ref=res.at[f, :, pl.ds(pl.multiple_of(HALF * o, HALF), HALF)],
            send_sem=res_send.at[f], recv_sem=res_recv.at[f],
            device_id=partner, device_id_type=MESH,
        )

    def hand_main():
        return pltpu.make_async_remote_copy(
            src_ref=hand_out, dst_ref=hand_in, send_sem=hand_send.at[0], recv_sem=hand_recv.at[0],
            device_id=(h, space), device_id_type=MESH,
        )

    def hand_side():
        return pltpu.make_async_remote_copy(
            src_ref=hand_out.at[:, :, pl.ds(pl.multiple_of(SIDE * h, SIDE), SIDE)], dst_ref=side_in,
            send_sem=hand_send.at[1], recv_sem=hand_recv.at[1],
            device_id=(o, at_space(2 * h - 1)), device_id_type=MESH,
        )

    def relay():
        return pltpu.make_async_remote_copy(
            src_ref=hand_in.at[:, :, pl.ds(pl.multiple_of(SIDE * o, SIDE), SIDE)], dst_ref=relay_in,
            send_sem=hand_send.at[2], recv_sem=hand_recv.at[2],
            device_id=partner, device_id_type=MESH,
        )

    wait_chunk(1, OPS)
    coefficients(1)

    @pl.when(pair == 1)
    def _():
        wait_chunk(1, 3)
        for t in range(T):
            for p in range(2):
                r[t + 1, p] = fr[1, 3, :, p, frame(t), :]

    @pl.when(pair == 0)
    def _():
        hand_main().wait_recv()
        relay().start()
        adj[0, :, :, SIDE:SIDE + HALF] = hand_in[...].astype(jnp.float32)
        hand_side().wait_recv()
        adj[0, :, :, pl.ds(pl.multiple_of((SIDE + HALF) * h, SIDE), SIDE)] = side_in[...].astype(jnp.float32)
        relay().wait_recv()
        adj[0, :, :, pl.ds(pl.multiple_of((SIDE + HALF) * o, SIDE), SIDE)] = relay_in[...].astype(jnp.float32)
        for t in range(T):
            for p in range(2):
                r[t + 1, p] = adj[0, :, p, adj_frame(t), :]

    pads(r)
    steps(1, pair)
    to_adj(0)

    @pl.when(h == 0)
    def _():
        for f in range(F):
            result_copy(0, f).start()

    wait_chunk(0, OPS)
    coefficients(0)
    steps(0, 0)
    to_adj(1)

    @pl.when(pair == 1)
    def _():
        hand_out[...] = adj[1, :, :, SIDE:SIDE + HALF].astype(jnp.bfloat16)
        hand_side().start()
        hand_main().start()

    @pl.when(h == 1)
    def _():
        for f in range(F):
            result_copy(1, f).start()

    def out_copy(f):
        return pltpu.make_async_copy(outv.at[f], out.at[0, f], out_sem.at[f])

    own = adj.at[1 - h]
    res[:, :, pl.ds(pl.multiple_of(HALF * h, HALF), HALF)] = own[:, :, SIDE:SIDE + HALF]
    for f in range(F):
        result_arrival(f).wait_recv()
        for p in range(2):
            outv[f, pl.ds(p, 128, stride=2), :] = (1.0 / OMEGA) * jnp.transpose(res[f, p])
        out_copy(f).start()

    for c in range(STEPS + 1):
        partner_copy(c).wait_send()
    for slot in range(2):
        @pl.when(h == slot)
        def _(slot=slot):
            for c in range(STEPS + 1):
                for copy in ext_copies(slot, c):
                    copy.wait_send()

    cp_copy(h).wait_send()
    for f in range(F):
        result_copy(0, f).wait_send()

    @pl.when(pair == 1)
    def _():
        hand_main().wait_send()
        hand_side().wait_send()

    @pl.when(pair == 0)
    def _():
        relay().wait_send()

    for f in range(F):
        out_copy(f).wait()


def per_device(forcing, zonal_courant, meridional_courant, zonal_faces, meridional_faces, coupling):
    f32, bf16 = jnp.float32, jnp.bfloat16
    dma = pltpu.SemaphoreType.DMA
    state = pltpu.VMEM((T + 2, 2, F, 8, 128), f32)
    return pl.pallas_call(
        body,
        out_shape=jax.ShapeDtypeStruct((1,) + forcing.shape[2:], f32),
        in_specs=[pl.BlockSpec(memory_space=pl.ANY)] * 6,
        out_specs=pl.BlockSpec(memory_space=pl.ANY),
        scratch_shapes=[
            pltpu.VMEM((STEPS, F, 256, 128), bf16),
            pltpu.VMEM((4, 256, 128), f32),
            pltpu.VMEM((256, 128), f32),
            pltpu.VMEM((2, STEPS, F, 2, ROWS, 128), f32),
            pltpu.VMEM((2, 4, 2, ROWS, 128), f32),
            pltpu.VMEM((2, F, 1, F), f32),
            pltpu.VMEM((2, T + 2, 2, 8, 128), f32),
            pltpu.VMEM((T, 2, 9, 8, 128), f32),
            pltpu.VMEM((F, F, 8, 128), f32),
            state, state, state,
            pltpu.VMEM((2, F, 2, HALF + 2 * SIDE, 128), f32),
            pltpu.VMEM((F, 2, HALF, 128), bf16),
            pltpu.VMEM((F, 2, HALF, 128), bf16),
            pltpu.VMEM((F, 2, SIDE, 128), bf16),
            pltpu.VMEM((F, 2, SIDE, 128), bf16),
            pltpu.VMEM((F, 2, WIDTH, 128), f32),
            pltpu.VMEM((F, 256, 128), f32),
            dma((9,)), dma((F,)),
            dma((6,)), dma((6,)),
            dma((2, 5)), dma((2, 5)),
            dma((3,)), dma((3,)),
            dma((F,)), dma((F,)),
        ],
        compiler_params=pltpu.CompilerParams(
            collective_id=0, has_side_effects=True, vmem_limit_bytes=60 * 1024 * 1024
        ),
        name="adjoint_window",
    )(forcing, zonal_courant, meridional_courant, zonal_faces, meridional_faces, jnp.transpose(coupling, (1, 0, 2)))


def solution(mesh):
    return jax.shard_map(
        per_device,
        mesh=mesh,
        in_specs=(
            P("tm", None, None, None, "space"),
            P("tm", None, "space"),
            P("tm", None, "space"),
            P("tm", None, "space"),
            P("tm", None, "space"),
            P("tm", None, None),
        ),
        out_specs=P("tm", None, None, "space"),
        check_vma=False,
    )
```

```python
import jax
import jax.numpy as jnp
from jax import lax
from jax.experimental import pallas as pl
from jax.experimental.pallas import tpu as pltpu
from jax.sharding import PartitionSpec as P

OMEGA = 0.4
STEPS = 4
F = 6
WIDTH = 128
HALF = 64
HALO = 24
SIDE = 32
TS = (11, 14)
T = max(TS)
WEST = (12, 24)
ROWS = WIDTH + 2 * HALO
OPS = STEPS
EXT = ((0, 8, 8, 16, 16), (16, 16, 24, 24, 24))
MESH = pl.DeviceIdType.MESH
UNROLL = True


def body(
    forcing, courant_x, courant_y, faces_x, faces_y, coupling, out,
    nat_f, nat_o, even_odd, fr, op, cp, ops, ext_out, ext_in,
    co, mix, r, x1, x2, r_n, x1_n, x2_n, adj, hand_out, hand_in, side_in, relay_in, res, outv,
    load_sem, out_sem, part_send, part_recv, ext_send, ext_recv,
    hand_send, hand_recv, res_send, res_recv,
):
    tm = lax.axis_index("tm")
    space = lax.axis_index("space")
    n_space = lax.axis_size("space")
    h = lax.rem(tm, 2)
    o = 1 - h
    pair = tm // 2

    def at_space(d):
        return lax.rem(space + d + n_space, n_space)

    barrier = pltpu.get_barrier_semaphore()
    count = 0
    for d in (-1, 1, 0):
        for j in range(4):
            if d == 0 and j == 0:
                continue
            other = lax.rem(tm + j, 4)
            pl.semaphore_signal(barrier, inc=1, device_id=(other, at_space(d)), device_id_type=MESH)
            count += 1

    ops_in = (faces_x, faces_y, courant_x, courant_y)
    loads = [pltpu.make_async_copy(ops_in[i].at[0], nat_o.at[i], load_sem.at[i]) for i in range(4)]
    loads.append(pltpu.make_async_copy(coupling, cp.at[h], load_sem.at[4]))
    loads += [pltpu.make_async_copy(forcing.at[0, k], nat_f.at[k], load_sem.at[5 + k]) for k in range(STEPS)]
    for i in (0, 1, 2, 3, 8, 4, 7, 6, 5):
        loads[i].start()

    partner = (2 * pair + o, space)
    to_east = (2 * pair, at_space(1))
    to_west = (2 * pair + 1, at_space(-1))

    def chunk(slot, c):
        return op.at[slot] if c == OPS else fr.at[slot, c]

    def partner_copy(c):
        ref = chunk(h, c).at[:, :, pl.ds(pl.multiple_of(HALO + 40 * o, 8), 88)]
        return pltpu.make_async_remote_copy(
            src_ref=ref, dst_ref=ref, send_sem=part_send.at[c], recv_sem=part_recv.at[c],
            device_id=partner, device_id_type=MESH,
        )

    def partner_arrival(c):
        ref = chunk(o, c).at[:, :, pl.ds(pl.multiple_of(HALO + 40 * h, 8), 88)]
        return pltpu.make_async_remote_copy(
            src_ref=ref, dst_ref=ref, send_sem=part_send.at[c], recv_sem=part_recv.at[c],
            device_id=partner, device_id_type=MESH,
        )

    def ext_ends(slot, c, side):
        n = EXT[slot][c]
        if c == OPS:
            start = (HALO + WIDTH - n, HALO)[side]
            there = (HALO - n, HALO + WIDTH)[side]
            return op.at[slot, :, :, pl.ds(start, n)], op.at[slot, :, :, pl.ds(there, n)]
        return ext_out.at[side, c, :, pl.ds(0, 2 * n)], ext_in.at[slot, c, :, pl.ds(0, 2 * n)]

    def ext_pack(slot, c):
        n = EXT[slot][c]
        if c < OPS and n:
            for side in range(2):
                start = (HALO + WIDTH - n, HALO)[side]
                both = jnp.concatenate([fr[slot, c, :, p, start:start + n] for p in range(2)], axis=1)
                ext_out[side, c, :, 0:2 * n] = both.astype(jnp.bfloat16)

    def ext_copies(slot, c):
        if EXT[slot][c] == 0:
            return []
        copies = []
        for side in range(2):
            src, dst = ext_ends(slot, c, side)
            copies.append(pltpu.make_async_remote_copy(
                src_ref=src, dst_ref=dst,
                send_sem=ext_send.at[side, c], recv_sem=ext_recv.at[slot, c],
                device_id=(to_east, to_west)[side], device_id_type=MESH,
            ))
        return copies

    def ext_arrival(slot, c):
        n = EXT[slot][c]
        start = pl.multiple_of((HALO - n) * o + (HALO + WIDTH) * h, 8)
        if c == OPS:
            ref = op.at[slot, :, :, pl.ds(start, n)]
        else:
            ref = ext_in.at[slot, c, :, pl.ds(0, 2 * n)]
        pltpu.make_async_remote_copy(
            src_ref=ref, dst_ref=ref, send_sem=ext_send.at[0, c], recv_sem=ext_recv.at[slot, c],
            device_id=to_east, device_id_type=MESH,
        ).wait_recv()
        if c < OPS:
            both = ext_in[slot, c, :, 0:2 * n].astype(jnp.float32)
            for p in range(2):
                fr[slot, c, :, p, pl.ds(start, n)] = both[:, p * n:(p + 1) * n]

    def wait_chunk(slot, c):
        @pl.when(h != slot)
        def _():
            partner_arrival(c).wait_recv()

        if EXT[slot][c]:
            ext_arrival(slot, c)

    def cp_copy(slot):
        return pltpu.make_async_remote_copy(
            src_ref=cp.at[slot], dst_ref=cp.at[slot],
            send_sem=part_send.at[5], recv_sem=part_recv.at[5],
            device_id=partner, device_id_type=MESH,
        )

    for slot in range(2):
        for c in range(STEPS + 1):
            n = EXT[slot][c]
            if n < HALO:
                ref = chunk(slot, c)
                start = pl.multiple_of((HALO + WIDTH + n) * h, 8)
                ref[:, :, pl.ds(start, HALO - n)] = jnp.zeros(ref.shape[:2] + (HALO - n, 128), jnp.float32)

    for i in range(4):
        loads[i].wait()
    for i in range(4):
        for p in range(2):
            op[h, i, p, HALO:HALO + WIDTH] = jnp.transpose(nat_o[i, pl.ds(p, 128, stride=2), :])
    pl.semaphore_wait(barrier, count)

    def send_first(c):
        @pl.when(h == 1)
        def _():
            ext_pack(1, c)
            for copy in ext_copies(1, c):
                copy.start()

        partner_copy(c).start()

    send_first(OPS)
    for k in (3, 2, 1, 0):
        loads[5 + k].wait()

        def one(f, carry, k=k):
            even_odd[...] = nat_f[k, f].astype(jnp.float32)
            for p in range(2):
                fr[h, k, f, p, HALO:HALO + WIDTH] = jnp.transpose(even_odd[pl.ds(p, 128, stride=2), :])
            return carry

        lax.fori_loop(0, F, one, 0)
        send_first(k)
        if k == 3:
            loads[4].wait()
            cp_copy(h).start()

    @pl.when(h == 0)
    def _():
        for c in (OPS, 3, 2, 1, 0):
            ext_pack(0, c)
            for copy in ext_copies(0, c):
                copy.start()

    lane = lax.broadcasted_iota(jnp.int32, (8, 128), 1)

    def frame(slot, t):
        return pl.ds(HALF * h + HALO - WEST[slot] + t, 8, stride=TS[slot])

    def coefficients(slot):
        @pl.when(h != slot)
        def _():
            cp_copy(o).wait_recv()

        last = TS[slot]
        for g in range(F):
            row = cp[slot, g]
            for f in range(F):
                value = jnp.broadcast_to(row[:, f:f + 1], (8, 128))
                mix[slot, g, f] = OMEGA * (value + 1.0) if g == f else OMEGA * value

        for i in (0, 2):
            for p in range(2):
                for t in range(last):
                    ops[i // 2, t + 1, p] = op[slot, i, p, frame(slot, t), :]
                ops[i // 2, 0, p] = pltpu.roll(ops[i // 2, last, p], 1, 0)
                ops[i // 2, last + 1, p] = pltpu.roll(ops[i // 2, 1, p], 7, 0)

        def one(t, carry):
            def get(i, p):
                return op[slot, i, p, frame(slot, t), :]

            b0, b1 = OMEGA * get(1, 0), OMEGA * get(1, 1)
            v0, v1 = 0.5 * OMEGA * get(3, 0), 0.5 * OMEGA * get(3, 1)
            north = (b0, jnp.where(lane == 127, 0.0, b1))
            south = (jnp.where(lane == 0, 0.0, pltpu.roll(b1, 1, 1)), b0)
            v_north = (v1, jnp.where(lane == 127, 0.0, pltpu.roll(v0, 127, 1)))
            v_south = (jnp.where(lane == 0, 0.0, -pltpu.roll(v1, 1, 1)), -v0)
            for p in range(2):
                east, west = OMEGA * ops[0, t + 1, p], OMEGA * ops[0, t, p]
                co[slot, t, p, 0] = (1.0 - OMEGA) - (east + west + north[p] + south[p])
                co[slot, t, p, 1] = east
                co[slot, t, p, 2] = west
                co[slot, t, p, 3] = (south, north)[p][p]
                co[slot, t, p, 4] = (north, south)[p][p]
                co[slot, t, p, 5] = 0.5 * OMEGA * ops[1, t + 2, p]
                co[slot, t, p, 6] = -0.5 * OMEGA * ops[1, t, p]
                co[slot, t, p, 7] = (v_south, v_north)[p][p]
                co[slot, t, p, 8] = (v_north, v_south)[p][p]
            return carry

        lax.fori_loop(0, last, one, 0)

    def pads(slot, buf):
        for p in range(2):
            buf[0, p] = pltpu.roll(buf[TS[slot], p], 1, 1)
            buf[TS[slot] + 1, p] = pltpu.roll(buf[1, p], 7, 1)

    def store(dst, dst_n, t, p, value):
        dst[t + 1, p] = value
        dst_n[t + 1, 1 - p] = pltpu.roll(value, 1 if p else 127, 2)

    def sweep(slot, src, src_n, dst, dst_n, add):
        def one(t, carry):
            for p in range(2):
                diag = co[slot, t, p, 0]
                if add is None:
                    value = (diag + 1.0) * src[t + 1, p]
                else:
                    value = diag * src[t + 1, p] + add[t + 1, p]
                value = value + co[slot, t, p, 1] * src[t + 2, p] + co[slot, t, p, 2] * src[t, p]
                value = value + co[slot, t, p, 3] * src_n[t + 1, p] + co[slot, t, p, 4] * src[t + 1, 1 - p]
                store(dst, dst_n, t, p, value)
            return carry

        lax.fori_loop(0, TS[slot], one, 0, unroll=UNROLL)
        pads(slot, dst)

    def explicit(slot, k):
        def one(t, carry):
            for p in range(2):
                value = fr[slot, k, :, p, frame(slot, t), :]
                value = value + co[slot, t, p, 5] * x2[t + 2, p] + co[slot, t, p, 6] * x2[t, p]
                value = value + co[slot, t, p, 7] * x2_n[t + 1, p] + co[slot, t, p, 8] * x2[t + 1, 1 - p]
                for g in range(F):
                    value = value + mix[slot, g] * x2[t + 1, p, g]
                store(r, r_n, t, p, value)
            return carry

        lax.fori_loop(0, TS[slot], one, 0, unroll=UNROLL)
        pads(slot, r)

    def steps(slot, first):
        def one(n, carry):
            k = STEPS - 1 - n
            sweep(slot, r, r_n, x1, x1_n, None)
            sweep(slot, x1, x1_n, x2, x2_n, r)
            for c in range(STEPS):
                @pl.when((k == c) & (pair == 1))
                def _(c=c):
                    wait_chunk(slot, c)

            explicit(slot, k)
            return carry

        lax.fori_loop(first, STEPS, one, 0)

    def adj_frame(slot, t):
        return pl.ds(SIDE - WEST[slot] + t, 8, stride=TS[slot])

    def to_adj(slot):
        for t in range(TS[slot]):
            for p in range(2):
                adj[1 - slot, :, p, adj_frame(slot, t), :] = r[t + 1, p]

    def from_adj(slot):
        for t in range(TS[slot]):
            for p in range(2):
                store(r, r_n, t, p, adj[0, :, p, adj_frame(slot, t), :])
        pads(slot, r)

    def result_copy(phase, f):
        return pltpu.make_async_remote_copy(
            src_ref=adj.at[phase, f, :, pl.ds(SIDE, HALF)],
            dst_ref=res.at[f, :, pl.ds(pl.multiple_of(HALF * h, HALF), HALF)],
            send_sem=res_send.at[f], recv_sem=res_recv.at[f],
            device_id=partner, device_id_type=MESH,
        )

    def result_arrival(f):
        return pltpu.make_async_remote_copy(
            src_ref=adj.at[0, f, :, pl.ds(SIDE, HALF)],
            dst_ref=res.at[f, :, pl.ds(pl.multiple_of(HALF * o, HALF), HALF)],
            send_sem=res_send.at[f], recv_sem=res_recv.at[f],
            device_id=partner, device_id_type=MESH,
        )

    def hand_main():
        return pltpu.make_async_remote_copy(
            src_ref=hand_out, dst_ref=hand_in, send_sem=hand_send.at[0], recv_sem=hand_recv.at[0],
            device_id=(h, space), device_id_type=MESH,
        )

    def hand_side():
        return pltpu.make_async_remote_copy(
            src_ref=hand_out.at[:, :, pl.ds(pl.multiple_of(SIDE * h, SIDE), SIDE)], dst_ref=side_in,
            send_sem=hand_send.at[1], recv_sem=hand_recv.at[1],
            device_id=(o, at_space(2 * h - 1)), device_id_type=MESH,
        )

    def relay():
        return pltpu.make_async_remote_copy(
            src_ref=hand_in.at[:, :, pl.ds(pl.multiple_of(SIDE * o, SIDE), SIDE)], dst_ref=relay_in,
            send_sem=hand_send.at[2], recv_sem=hand_recv.at[2],
            device_id=partner, device_id_type=MESH,
        )

    wait_chunk(1, OPS)
    coefficients(1)

    @pl.when(pair == 1)
    def _():
        wait_chunk(1, 3)
        for t in range(TS[1]):
            for p in range(2):
                store(r, r_n, t, p, fr[1, 3, :, p, frame(1, t), :])
        pads(1, r)

    @pl.when(pair == 0)
    def _():
        wait_chunk(0, OPS)
        coefficients(0)
        for slot in (1, 0):
            for c in range(STEPS):
                wait_chunk(slot, c)
        hand_main().wait_recv()
        relay().start()
        adj[0, :, :, SIDE:SIDE + HALF] = hand_in[...].astype(jnp.float32)
        hand_side().wait_recv()
        adj[0, :, :, pl.ds(pl.multiple_of((SIDE + HALF) * h, SIDE), SIDE)] = side_in[...].astype(jnp.float32)
        relay().wait_recv()
        adj[0, :, :, pl.ds(pl.multiple_of((SIDE + HALF) * o, SIDE), SIDE)] = relay_in[...].astype(jnp.float32)
        from_adj(1)

    steps(1, pair)
    to_adj(1)

    @pl.when(h == 0)
    def _():
        for f in range(F):
            result_copy(0, f).start()

    @pl.when(pair == 1)
    def _():
        wait_chunk(0, OPS)
        coefficients(0)

    from_adj(0)
    steps(0, 0)
    to_adj(0)

    @pl.when(pair == 1)
    def _():
        hand_out[...] = adj[1, :, :, SIDE:SIDE + HALF].astype(jnp.bfloat16)
        hand_side().start()
        hand_main().start()

    @pl.when(h == 1)
    def _():
        for f in range(F):
            result_copy(1, f).start()

    def out_copy(f):
        return pltpu.make_async_copy(outv.at[f], out.at[0, f], out_sem.at[f])

    own = adj.at[1 - h]
    res[:, :, pl.ds(pl.multiple_of(HALF * h, HALF), HALF)] = own[:, :, SIDE:SIDE + HALF]
    for f in range(F):
        result_arrival(f).wait_recv()
        for p in range(2):
            outv[f, pl.ds(p, 128, stride=2), :] = jnp.transpose(res[f, p])
        out_copy(f).start()

    for c in range(STEPS + 1):
        partner_copy(c).wait_send()
    for slot in range(2):
        @pl.when(h == slot)
        def _(slot=slot):
            for c in range(STEPS + 1):
                for copy in ext_copies(slot, c):
                    copy.wait_send()

    cp_copy(h).wait_send()
    for f in range(F):
        result_copy(0, f).wait_send()

    @pl.when(pair == 1)
    def _():
        hand_main().wait_send()
        hand_side().wait_send()

    @pl.when(pair == 0)
    def _():
        relay().wait_send()

    for f in range(F):
        out_copy(f).wait()


def per_device(forcing, zonal_courant, meridional_courant, zonal_faces, meridional_faces, coupling):
    f32, bf16 = jnp.float32, jnp.bfloat16
    dma = pltpu.SemaphoreType.DMA
    state = pltpu.VMEM((T + 2, 2, F, 8, 128), f32)
    beside = pltpu.VMEM((T + 1, 2, F, 8, 128), f32)
    return pl.pallas_call(
        body,
        out_shape=jax.ShapeDtypeStruct((1,) + forcing.shape[2:], f32),
        in_specs=[pl.BlockSpec(memory_space=pl.ANY)] * 6,
        out_specs=pl.BlockSpec(memory_space=pl.ANY),
        scratch_shapes=[
            pltpu.VMEM((STEPS, F, 256, 128), bf16),
            pltpu.VMEM((4, 256, 128), f32),
            pltpu.VMEM((256, 128), f32),
            pltpu.VMEM((2, STEPS, F, 2, ROWS, 128), f32),
            pltpu.VMEM((2, 4, 2, ROWS, 128), f32),
            pltpu.VMEM((2, F, 1, F), f32),
            pltpu.VMEM((2, T + 2, 2, 8, 128), f32),
            pltpu.VMEM((2, STEPS, F, 2 * HALO, 128), bf16),
            pltpu.VMEM((2, STEPS, F, 2 * HALO, 128), bf16),
            pltpu.VMEM((2, T, 2, 9, 8, 128), f32),
            pltpu.VMEM((2, F, F, 8, 128), f32),
            state, state, state, beside, beside, beside,
            pltpu.VMEM((2, F, 2, HALF + 2 * SIDE, 128), f32),
            pltpu.VMEM((F, 2, HALF, 128), bf16),
            pltpu.VMEM((F, 2, HALF, 128), bf16),
            pltpu.VMEM((F, 2, SIDE, 128), bf16),
            pltpu.VMEM((F, 2, SIDE, 128), bf16),
            pltpu.VMEM((F, 2, WIDTH, 128), f32),
            pltpu.VMEM((F, 256, 128), f32),
            dma((9,)), dma((F,)),
            dma((6,)), dma((6,)),
            dma((2, 5)), dma((2, 5)),
            dma((3,)), dma((3,)),
            dma((F,)), dma((F,)),
        ],
        compiler_params=pltpu.CompilerParams(
            collective_id=0, has_side_effects=True, vmem_limit_bytes=60 * 1024 * 1024
        ),
        name="adjoint_window",
    )(forcing, zonal_courant, meridional_courant, zonal_faces, meridional_faces, jnp.transpose(coupling, (1, 0, 2)))


def solution(mesh):
    return jax.shard_map(
        per_device,
        mesh=mesh,
        in_specs=(
            P("tm", None, None, None, "space"),
            P("tm", None, "space"),
            P("tm", None, "space"),
            P("tm", None, "space"),
            P("tm", None, "space"),
            P("tm", None, None),
        ),
        out_specs=P("tm", None, None, "space"),
        check_vma=False,
    )
```

```python
import jax
import jax.numpy as jnp
from jax import lax
from jax.experimental import pallas as pl
from jax.experimental.pallas import tpu as pltpu
from jax.sharding import PartitionSpec as P

OMEGA = 0.4
STEPS = 4
F = 6
WIDTH = 128
HALF = 64
HALO = 24
SIDE = 32
TS = (11, 14)
T = max(TS)
WEST = (12, 24)
ROWS = WIDTH + 2 * HALO
OPS = STEPS
EXT = ((0, 8, 8, 16, 16), (16, 16, 24, 24, 24))
MESH = pl.DeviceIdType.MESH
UNROLL = True


def body(
    forcing, courant_x, courant_y, faces_x, faces_y, coupling, out,
    nat_f, nat_o, even_odd, fr, op, cp, ops, ext_out, ext_in,
    co, mix, r, x1, x2, r_n, x1_n, x2_n, adj, hand_out, hand_in, side_out, side_in, relay_in, res, outv,
    load_sem, out_sem, part_send, part_recv, ext_send, ext_recv,
    hand_send, hand_recv, res_send, res_recv,
):
    tm = lax.axis_index("tm")
    space = lax.axis_index("space")
    n_space = lax.axis_size("space")
    h = lax.rem(tm, 2)
    o = 1 - h
    pair = tm // 2

    def at_space(d):
        return lax.rem(space + d + n_space, n_space)

    barrier = pltpu.get_barrier_semaphore()
    count = 0
    for d in (-1, 1, 0):
        for j in range(4):
            if d == 0 and j == 0:
                continue
            other = lax.rem(tm + j, 4)
            pl.semaphore_signal(barrier, inc=1, device_id=(other, at_space(d)), device_id_type=MESH)
            count += 1

    ops_in = (faces_x, faces_y, courant_x, courant_y)
    loads = [pltpu.make_async_copy(ops_in[i].at[0], nat_o.at[i], load_sem.at[i]) for i in range(4)]
    loads.append(pltpu.make_async_copy(coupling, cp.at[h], load_sem.at[4]))
    loads += [pltpu.make_async_copy(forcing.at[0, k], nat_f.at[k], load_sem.at[5 + k]) for k in range(STEPS)]
    for i in (0, 1, 2, 3, 8, 4, 7, 6, 5):
        loads[i].start()

    partner = (2 * pair + o, space)
    to_east = (2 * pair, at_space(1))
    to_west = (2 * pair + 1, at_space(-1))

    def chunk(slot, c):
        return op.at[slot] if c == OPS else fr.at[slot, c]

    def partner_copy(c):
        ref = chunk(h, c).at[:, :, pl.ds(pl.multiple_of(HALO + 40 * o, 8), 88)]
        return pltpu.make_async_remote_copy(
            src_ref=ref, dst_ref=ref, send_sem=part_send.at[c], recv_sem=part_recv.at[c],
            device_id=partner, device_id_type=MESH,
        )

    def partner_arrival(c):
        ref = chunk(o, c).at[:, :, pl.ds(pl.multiple_of(HALO + 40 * h, 8), 88)]
        return pltpu.make_async_remote_copy(
            src_ref=ref, dst_ref=ref, send_sem=part_send.at[c], recv_sem=part_recv.at[c],
            device_id=partner, device_id_type=MESH,
        )

    def ext_pack(slot, c):
        n, ref = EXT[slot][c], chunk(slot, c)
        if n:
            for side in range(2):
                start = (HALO + WIDTH - n, HALO)[side]
                both = jnp.concatenate([ref[:, p, start:start + n] for p in range(2)], axis=1)
                ext_out[side, c, 0:both.shape[0], 0:2 * n] = both.astype(jnp.bfloat16)

    def ext_copies(slot, c):
        n, count = EXT[slot][c], chunk(slot, c).shape[0]
        if n == 0:
            return []
        return [
            pltpu.make_async_remote_copy(
                src_ref=ext_out.at[side, c, pl.ds(0, count), pl.ds(0, 2 * n)],
                dst_ref=ext_in.at[slot, c, pl.ds(0, count), pl.ds(0, 2 * n)],
                send_sem=ext_send.at[side, c], recv_sem=ext_recv.at[slot, c],
                device_id=(to_east, to_west)[side], device_id_type=MESH,
            )
            for side in range(2)
        ]

    def ext_start(slot, c):
        for copy in ext_copies(slot, c):
            copy.start()

    def ext_sent(slot, c):
        for copy in ext_copies(slot, c):
            copy.wait_send()

    def ext_arrival(slot, c):
        n, dest = EXT[slot][c], chunk(slot, c)
        ref = ext_in.at[slot, c, pl.ds(0, dest.shape[0]), pl.ds(0, 2 * n)]
        pltpu.make_async_remote_copy(
            src_ref=ref, dst_ref=ref, send_sem=ext_send.at[0, c], recv_sem=ext_recv.at[slot, c],
            device_id=to_east, device_id_type=MESH,
        ).wait_recv()
        start = pl.multiple_of((HALO - n) * o + (HALO + WIDTH) * h, 8)
        both = ext_in[slot, c, 0:dest.shape[0], 0:2 * n].astype(jnp.float32)
        for p in range(2):
            dest[:, p, pl.ds(start, n)] = both[:, p * n:(p + 1) * n]

    def wait_chunk(slot, c):
        @pl.when(h != slot)
        def _():
            partner_arrival(c).wait_recv()

        if EXT[slot][c]:
            ext_arrival(slot, c)

    def cp_copy(slot):
        return pltpu.make_async_remote_copy(
            src_ref=cp.at[slot], dst_ref=cp.at[slot],
            send_sem=part_send.at[5], recv_sem=part_recv.at[5],
            device_id=partner, device_id_type=MESH,
        )

    for slot in range(2):
        for c in range(STEPS + 1):
            n = EXT[slot][c]
            if n < HALO:
                ref = chunk(slot, c)
                start = pl.multiple_of((HALO + WIDTH + n) * h, 8)
                ref[:, :, pl.ds(start, HALO - n)] = jnp.zeros(ref.shape[:2] + (HALO - n, 128), jnp.float32)

    for i in range(4):
        loads[i].wait()
    for i in range(4):
        for p in range(2):
            op[h, i, p, HALO:HALO + WIDTH] = jnp.transpose(nat_o[i, pl.ds(p, 128, stride=2), :])
    pl.semaphore_wait(barrier, count)

    def send_chunk(c):
        partner_copy(c).start()
        for slot in range(2):
            @pl.when(h == slot)
            def _(slot=slot):
                ext_pack(slot, c)
                if slot == 1 and c >= 3:
                    ext_start(slot, c)

    send_chunk(OPS)
    for k in (3, 2, 1, 0):
        loads[5 + k].wait()

        def one(f, carry, k=k):
            even_odd[...] = nat_f[k, f].astype(jnp.float32)
            for p in range(2):
                fr[h, k, f, p, HALO:HALO + WIDTH] = jnp.transpose(even_odd[pl.ds(p, 128, stride=2), :])
            return carry

        lax.fori_loop(0, F, one, 0)
        send_chunk(k)
        if k == 3:
            loads[4].wait()
            cp_copy(h).start()

    @pl.when(h == 1)
    def _():
        ext_sent(1, OPS)
        ext_sent(1, 3)
        ext_start(1, 2)

    def second_halos():
        @pl.when(h == 0)
        def _():
            for c in (OPS, 3, 2, 1, 0):
                ext_start(0, c)

    lane = lax.broadcasted_iota(jnp.int32, (8, 128), 1)

    def frame(slot, t):
        return pl.ds(HALF * h + HALO - WEST[slot] + t, 8, stride=TS[slot])

    def coefficients(slot):
        @pl.when(h != slot)
        def _():
            cp_copy(o).wait_recv()

        last = TS[slot]
        for g in range(F):
            row = cp[slot, g]
            for f in range(F):
                value = jnp.broadcast_to(row[:, f:f + 1], (8, 128))
                mix[slot, g, f] = OMEGA * (value + 1.0) if g == f else OMEGA * value

        for i in (0, 2):
            for p in range(2):
                for t in range(last):
                    ops[i // 2, t + 1, p] = op[slot, i, p, frame(slot, t), :]
                ops[i // 2, 0, p] = pltpu.roll(ops[i // 2, last, p], 1, 0)
                ops[i // 2, last + 1, p] = pltpu.roll(ops[i // 2, 1, p], 7, 0)

        def one(t, carry):
            def get(i, p):
                return op[slot, i, p, frame(slot, t), :]

            b0, b1 = OMEGA * get(1, 0), OMEGA * get(1, 1)
            v0, v1 = 0.5 * OMEGA * get(3, 0), 0.5 * OMEGA * get(3, 1)
            north = (b0, jnp.where(lane == 127, 0.0, b1))
            south = (jnp.where(lane == 0, 0.0, pltpu.roll(b1, 1, 1)), b0)
            v_north = (v1, jnp.where(lane == 127, 0.0, pltpu.roll(v0, 127, 1)))
            v_south = (jnp.where(lane == 0, 0.0, -pltpu.roll(v1, 1, 1)), -v0)
            for p in range(2):
                east, west = OMEGA * ops[0, t + 1, p], OMEGA * ops[0, t, p]
                co[slot, t, p, 0] = (1.0 - OMEGA) - (east + west + north[p] + south[p])
                co[slot, t, p, 1] = east
                co[slot, t, p, 2] = west
                co[slot, t, p, 3] = (south, north)[p][p]
                co[slot, t, p, 4] = (north, south)[p][p]
                co[slot, t, p, 5] = 0.5 * OMEGA * ops[1, t + 2, p]
                co[slot, t, p, 6] = -0.5 * OMEGA * ops[1, t, p]
                co[slot, t, p, 7] = (v_south, v_north)[p][p]
                co[slot, t, p, 8] = (v_north, v_south)[p][p]
            return carry

        lax.fori_loop(0, last, one, 0)

    def pads(slot, buf):
        for p in range(2):
            buf[0, p] = pltpu.roll(buf[TS[slot], p], 1, 1)
            buf[TS[slot] + 1, p] = pltpu.roll(buf[1, p], 7, 1)

    def store(dst, dst_n, t, p, value):
        dst[t + 1, p] = value
        dst_n[t + 1, 1 - p] = pltpu.roll(value, 1 if p else 127, 2)

    def sweep(slot, src, src_n, dst, dst_n, add):
        def one(t, carry):
            for p in range(2):
                diag = co[slot, t, p, 0]
                if add is None:
                    value = (diag + 1.0) * src[t + 1, p]
                else:
                    value = diag * src[t + 1, p] + add[t + 1, p]
                value = value + co[slot, t, p, 1] * src[t + 2, p] + co[slot, t, p, 2] * src[t, p]
                value = value + co[slot, t, p, 3] * src_n[t + 1, p] + co[slot, t, p, 4] * src[t + 1, 1 - p]
                store(dst, dst_n, t, p, value)
            return carry

        lax.fori_loop(0, TS[slot], one, 0, unroll=UNROLL)
        pads(slot, dst)

    def explicit(slot, k):
        def one(t, carry):
            for p in range(2):
                value = fr[slot, k, :, p, frame(slot, t), :]
                value = value + co[slot, t, p, 5] * x2[t + 2, p] + co[slot, t, p, 6] * x2[t, p]
                value = value + co[slot, t, p, 7] * x2_n[t + 1, p] + co[slot, t, p, 8] * x2[t + 1, 1 - p]
                for g in range(F):
                    value = value + mix[slot, g] * x2[t + 1, p, g]
                store(r, r_n, t, p, value)
            return carry

        lax.fori_loop(0, TS[slot], one, 0, unroll=UNROLL)
        pads(slot, r)

    def steps(slot, first):
        def one(n, carry):
            k = STEPS - 1 - n
            sweep(slot, r, r_n, x1, x1_n, None)
            sweep(slot, x1, x1_n, x2, x2_n, r)
            for c in range(STEPS):
                @pl.when((k == c) & (pair == 1))
                def _(c=c):
                    wait_chunk(slot, c)
                    if slot == 1 and c == 2:
                        second_halos()

            explicit(slot, k)
            return carry

        lax.fori_loop(first, STEPS, one, 0)

    def adj_frame(slot, t):
        return pl.ds(SIDE - WEST[slot] + t, 8, stride=TS[slot])

    def to_adj(slot):
        for t in range(TS[slot]):
            for p in range(2):
                adj[1 - slot, :, p, adj_frame(slot, t), :] = r[t + 1, p]

    def from_adj(slot):
        for t in range(TS[slot]):
            for p in range(2):
                store(r, r_n, t, p, adj[0, :, p, adj_frame(slot, t), :])
        pads(slot, r)

    def result_copy(phase, f):
        return pltpu.make_async_remote_copy(
            src_ref=adj.at[phase, f, :, pl.ds(SIDE, HALF)],
            dst_ref=res.at[f, :, pl.ds(pl.multiple_of(HALF * h, HALF), HALF)],
            send_sem=res_send.at[f], recv_sem=res_recv.at[f],
            device_id=partner, device_id_type=MESH,
        )

    def result_arrival(f):
        return pltpu.make_async_remote_copy(
            src_ref=adj.at[0, f, :, pl.ds(SIDE, HALF)],
            dst_ref=res.at[f, :, pl.ds(pl.multiple_of(HALF * o, HALF), HALF)],
            send_sem=res_send.at[f], recv_sem=res_recv.at[f],
            device_id=partner, device_id_type=MESH,
        )

    def hand_main(f):
        return pltpu.make_async_remote_copy(
            src_ref=hand_out.at[f], dst_ref=hand_in.at[f], send_sem=hand_send.at[f], recv_sem=hand_recv.at[f],
            device_id=(h, space), device_id_type=MESH,
        )

    def hand_side():
        return pltpu.make_async_remote_copy(
            src_ref=side_out, dst_ref=side_in, send_sem=hand_send.at[F], recv_sem=hand_recv.at[F],
            device_id=(o, at_space(2 * h - 1)), device_id_type=MESH,
        )

    def relay(f):
        return pltpu.make_async_remote_copy(
            src_ref=hand_in.at[f, :, pl.ds(pl.multiple_of(SIDE * o, SIDE), SIDE)], dst_ref=relay_in.at[f],
            send_sem=hand_send.at[F + 1 + f], recv_sem=hand_recv.at[F + 1 + f],
            device_id=partner, device_id_type=MESH,
        )

    wait_chunk(1, OPS)
    coefficients(1)

    @pl.when(h == 1)
    def _():
        ext_sent(1, 2)
        ext_start(1, 1)
        ext_start(1, 0)

    @pl.when(pair == 1)
    def _():
        wait_chunk(1, 3)
        for t in range(TS[1]):
            for p in range(2):
                store(r, r_n, t, p, fr[1, 3, :, p, frame(1, t), :])
        pads(1, r)

    @pl.when(pair == 0)
    def _():
        second_halos()
        for c in range(STEPS):
            wait_chunk(1, c)
        wait_chunk(0, OPS)
        coefficients(0)
        for c in range(STEPS):
            wait_chunk(0, c)
        for f in range(F):
            hand_main(f).wait_recv()
            relay(f).start()
            adj[0, f, :, SIDE:SIDE + HALF] = hand_in[f].astype(jnp.float32)
        hand_side().wait_recv()
        both = side_in[...].astype(jnp.float32)
        for p in range(2):
            start = pl.multiple_of((SIDE - HALO) * o + (SIDE + HALF) * h, 8)
            adj[0, :, p, pl.ds(start, HALO)] = both[:, p * HALO:(p + 1) * HALO]
        for f in range(F):
            relay(f).wait_recv()
            adj[0, f, :, pl.ds(pl.multiple_of((SIDE + HALF) * o, SIDE), SIDE)] = relay_in[f].astype(jnp.float32)
        from_adj(1)

    steps(1, pair)
    to_adj(1)

    @pl.when(h == 0)
    def _():
        for f in range(F):
            result_copy(0, f).start()

    @pl.when(pair == 1)
    def _():
        wait_chunk(0, OPS)
        coefficients(0)

    from_adj(0)
    steps(0, 0)
    to_adj(0)

    @pl.when(pair == 1)
    def _():
        start = pl.multiple_of(SIDE + (HALF - HALO) * h, 8)
        both = jnp.concatenate([adj[1, :, p, pl.ds(start, HALO)] for p in range(2)], axis=1)
        side_out[...] = both.astype(jnp.bfloat16)
        hand_side().start()
        for f in range(F):
            hand_out[f] = adj[1, f, :, SIDE:SIDE + HALF].astype(jnp.bfloat16)
            hand_main(f).start()

    @pl.when(h == 1)
    def _():
        for f in range(F):
            result_copy(1, f).start()

    def out_copy(f):
        return pltpu.make_async_copy(outv.at[f], out.at[0, f], out_sem.at[f])

    own = adj.at[1 - h]
    res[:, :, pl.ds(pl.multiple_of(HALF * h, HALF), HALF)] = own[:, :, SIDE:SIDE + HALF]
    for f in range(F):
        result_arrival(f).wait_recv()
        for p in range(2):
            outv[f, pl.ds(p, 128, stride=2), :] = jnp.transpose(res[f, p])
        out_copy(f).start()

    for c in range(STEPS + 1):
        partner_copy(c).wait_send()
    for slot, left in ((0, (OPS, 3, 2, 1)), (1, (1, 0))):
        @pl.when(h == slot)
        def _(slot=slot, left=left):
            for c in left:
                ext_sent(slot, c)

    cp_copy(h).wait_send()
    for f in range(F):
        result_copy(0, f).wait_send()

    @pl.when(pair == 1)
    def _():
        hand_side().wait_send()
        for f in range(F):
            hand_main(f).wait_send()

    @pl.when(pair == 0)
    def _():
        for f in range(F):
            relay(f).wait_send()

    for f in range(F):
        out_copy(f).wait()


def per_device(forcing, zonal_courant, meridional_courant, zonal_faces, meridional_faces, coupling):
    f32, bf16 = jnp.float32, jnp.bfloat16
    dma = pltpu.SemaphoreType.DMA
    state = pltpu.VMEM((T + 2, 2, F, 8, 128), f32)
    beside = pltpu.VMEM((T + 1, 2, F, 8, 128), f32)
    return pl.pallas_call(
        body,
        out_shape=jax.ShapeDtypeStruct((1,) + forcing.shape[2:], f32),
        in_specs=[pl.BlockSpec(memory_space=pl.ANY)] * 6,
        out_specs=pl.BlockSpec(memory_space=pl.ANY),
        scratch_shapes=[
            pltpu.VMEM((STEPS, F, 256, 128), bf16),
            pltpu.VMEM((4, 256, 128), f32),
            pltpu.VMEM((256, 128), f32),
            pltpu.VMEM((2, STEPS, F, 2, ROWS, 128), f32),
            pltpu.VMEM((2, 4, 2, ROWS, 128), f32),
            pltpu.VMEM((2, F, 1, F), f32),
            pltpu.VMEM((2, T + 2, 2, 8, 128), f32),
            pltpu.VMEM((2, STEPS + 1, F, 2 * HALO, 128), bf16),
            pltpu.VMEM((2, STEPS + 1, F, 2 * HALO, 128), bf16),
            pltpu.VMEM((2, T, 2, 9, 8, 128), f32),
            pltpu.VMEM((2, F, F, 8, 128), f32),
            state, state, state, beside, beside, beside,
            pltpu.VMEM((2, F, 2, HALF + 2 * SIDE, 128), f32),
            pltpu.VMEM((F, 2, HALF, 128), bf16),
            pltpu.VMEM((F, 2, HALF, 128), bf16),
            pltpu.VMEM((F, 2 * HALO, 128), bf16),
            pltpu.VMEM((F, 2 * HALO, 128), bf16),
            pltpu.VMEM((F, 2, SIDE, 128), bf16),
            pltpu.VMEM((F, 2, WIDTH, 128), f32),
            pltpu.VMEM((F, 256, 128), f32),
            dma((9,)), dma((F,)),
            dma((6,)), dma((6,)),
            dma((2, 5)), dma((2, 5)),
            dma((2 * F + 1,)), dma((2 * F + 1,)),
            dma((F,)), dma((F,)),
        ],
        compiler_params=pltpu.CompilerParams(
            collective_id=0, has_side_effects=True, vmem_limit_bytes=60 * 1024 * 1024
        ),
        name="adjoint_window",
    )(forcing, zonal_courant, meridional_courant, zonal_faces, meridional_faces, jnp.transpose(coupling, (1, 0, 2)))


def solution(mesh):
    return jax.shard_map(
        per_device,
        mesh=mesh,
        in_specs=(
            P("tm", None, None, None, "space"),
            P("tm", None, "space"),
            P("tm", None, "space"),
            P("tm", None, "space"),
            P("tm", None, "space"),
            P("tm", None, None),
        ),
        out_specs=P("tm", None, None, "space"),
        check_vma=False,
    )
```

```python
import jax
import jax.numpy as jnp
from jax import lax
from jax.experimental import pallas as pl
from jax.experimental.pallas import tpu as pltpu
from jax.sharding import PartitionSpec as P

OMEGA = 0.4
STEPS = 4
F = 6
WIDTH = 128
HALF = 64
HALO = 24
SIDE = 32
TS = (11, 14)
T = max(TS)
WEST = (12, 24)
ROWS = WIDTH + 2 * HALO
OPS = STEPS
EXT = ((0, 8, 8, 16, 16), (16, 16, 24, 24, 24))
MESH = pl.DeviceIdType.MESH
UNROLL = True


def body(
    forcing, courant_x, courant_y, faces_x, faces_y, coupling, out,
    nat_f, nat_o, even_odd, fr, op, cp, ops, ext_out, ext_in,
    co, mix, r, x1, x2, r_n, x1_n, x2_n, adj, hand_out, hand_in, side_out, side_in, relay_in, res, outv,
    load_sem, out_sem, part_send, part_recv, ext_send, ext_recv,
    hand_send, hand_recv, res_send, res_recv,
):
    tm = lax.axis_index("tm")
    space = lax.axis_index("space")
    n_space = lax.axis_size("space")
    h = lax.rem(tm, 2)
    o = 1 - h
    pair = tm // 2

    def at_space(d):
        return lax.rem(space + d + n_space, n_space)

    barrier = pltpu.get_barrier_semaphore()
    count = 0
    for d in (-1, 1, 0):
        for j in range(4):
            if d == 0 and j == 0:
                continue
            other = lax.rem(tm + j, 4)
            pl.semaphore_signal(barrier, inc=1, device_id=(other, at_space(d)), device_id_type=MESH)
            count += 1

    ops_in = (faces_x, faces_y, courant_x, courant_y)
    loads = [pltpu.make_async_copy(ops_in[i].at[0], nat_o.at[i], load_sem.at[i]) for i in range(4)]
    loads.append(pltpu.make_async_copy(coupling, cp.at[h], load_sem.at[4]))
    loads += [pltpu.make_async_copy(forcing.at[0, k], nat_f.at[k], load_sem.at[5 + k]) for k in range(STEPS)]
    for i in (0, 1, 2, 3, 8, 4, 7, 6, 5):
        loads[i].start()

    partner = (2 * pair + o, space)
    to_east = (2 * pair, at_space(1))
    to_west = (2 * pair + 1, at_space(-1))

    def chunk(slot, c):
        return op.at[slot] if c == OPS else fr.at[slot, c]

    def partner_copy(c):
        ref = chunk(h, c).at[:, :, pl.ds(pl.multiple_of(HALO + 40 * o, 8), 88)]
        return pltpu.make_async_remote_copy(
            src_ref=ref, dst_ref=ref, send_sem=part_send.at[c], recv_sem=part_recv.at[c],
            device_id=partner, device_id_type=MESH,
        )

    def partner_arrival(c):
        ref = chunk(o, c).at[:, :, pl.ds(pl.multiple_of(HALO + 40 * h, 8), 88)]
        return pltpu.make_async_remote_copy(
            src_ref=ref, dst_ref=ref, send_sem=part_send.at[c], recv_sem=part_recv.at[c],
            device_id=partner, device_id_type=MESH,
        )

    def ext_pack(slot, c):
        n, ref = EXT[slot][c], chunk(slot, c)
        if n:
            for side in range(2):
                start = (HALO + WIDTH - n, HALO)[side]
                both = jnp.concatenate([ref[:, p, start:start + n] for p in range(2)], axis=1)
                ext_out[side, c, 0:both.shape[0], 0:2 * n] = both.astype(jnp.bfloat16)

    def ext_copies(slot, c):
        n, count = EXT[slot][c], chunk(slot, c).shape[0]
        if n == 0:
            return []
        return [
            pltpu.make_async_remote_copy(
                src_ref=ext_out.at[side, c, pl.ds(0, count), pl.ds(0, 2 * n)],
                dst_ref=ext_in.at[slot, c, pl.ds(0, count), pl.ds(0, 2 * n)],
                send_sem=ext_send.at[side, c], recv_sem=ext_recv.at[slot, c],
                device_id=(to_east, to_west)[side], device_id_type=MESH,
            )
            for side in range(2)
        ]

    def ext_start(slot, c):
        for copy in ext_copies(slot, c):
            copy.start()

    def ext_sent(slot, c):
        for copy in ext_copies(slot, c):
            copy.wait_send()

    def ext_arrival(slot, c):
        n, dest = EXT[slot][c], chunk(slot, c)
        ref = ext_in.at[slot, c, pl.ds(0, dest.shape[0]), pl.ds(0, 2 * n)]
        pltpu.make_async_remote_copy(
            src_ref=ref, dst_ref=ref, send_sem=ext_send.at[0, c], recv_sem=ext_recv.at[slot, c],
            device_id=to_east, device_id_type=MESH,
        ).wait_recv()
        start = pl.multiple_of((HALO - n) * o + (HALO + WIDTH) * h, 8)
        both = ext_in[slot, c, 0:dest.shape[0], 0:2 * n].astype(jnp.float32)
        for p in range(2):
            dest[:, p, pl.ds(start, n)] = both[:, p * n:(p + 1) * n]

    def wait_chunk(slot, c):
        @pl.when(h != slot)
        def _():
            partner_arrival(c).wait_recv()

        if EXT[slot][c]:
            ext_arrival(slot, c)

    def cp_copy(slot):
        return pltpu.make_async_remote_copy(
            src_ref=cp.at[slot], dst_ref=cp.at[slot],
            send_sem=part_send.at[5], recv_sem=part_recv.at[5],
            device_id=partner, device_id_type=MESH,
        )

    for slot in range(2):
        for c in range(STEPS + 1):
            n = EXT[slot][c]
            if n < HALO:
                ref = chunk(slot, c)
                start = pl.multiple_of((HALO + WIDTH + n) * h, 8)
                ref[:, :, pl.ds(start, HALO - n)] = jnp.zeros(ref.shape[:2] + (HALO - n, 128), jnp.float32)

    for i in range(4):
        loads[i].wait()
    for i in range(4):
        for p in range(2):
            op[h, i, p, HALO:HALO + WIDTH] = jnp.transpose(nat_o[i, pl.ds(p, 128, stride=2), :])
    def send_chunk(c):
        partner_copy(c).start()
        for slot in range(2):
            @pl.when(h == slot)
            def _(slot=slot):
                ext_pack(slot, c)
                if slot == 1:
                    ext_start(slot, c)

    early = lax.rem(space, 16) == 0

    @pl.when(jnp.logical_not(early))
    def _():
        pl.semaphore_wait(barrier, count)
        send_chunk(OPS)

    for k in (3, 2, 1, 0):
        loads[5 + k].wait()

        def one(f, carry, k=k):
            even_odd[...] = nat_f[k, f].astype(jnp.float32)
            for p in range(2):
                fr[h, k, f, p, HALO:HALO + WIDTH] = jnp.transpose(even_odd[pl.ds(p, 128, stride=2), :])
            return carry

        lax.fori_loop(0, F, one, 0)

        @pl.when(jnp.logical_not(early))
        def _(k=k):
            send_chunk(k)

    @pl.when(early)
    def _():
        pl.semaphore_wait(barrier, count)
        for c in (OPS, 3, 2, 1, 0):
            send_chunk(c)

    loads[4].wait()
    cp_copy(h).start()

    @pl.when(h == 0)
    def _():
        for c in (OPS, 3, 2, 1, 0):
            ext_start(0, c)

    lane = lax.broadcasted_iota(jnp.int32, (8, 128), 1)

    def frame(slot, t):
        return pl.ds(HALF * h + HALO - WEST[slot] + t, 8, stride=TS[slot])

    def coefficients(slot):
        @pl.when(h != slot)
        def _():
            cp_copy(o).wait_recv()

        last = TS[slot]
        for g in range(F):
            row = cp[slot, g]
            for f in range(F):
                value = jnp.broadcast_to(row[:, f:f + 1], (8, 128))
                mix[slot, g, f] = OMEGA * (value + 1.0) if g == f else OMEGA * value

        for i in (0, 2):
            for p in range(2):
                for t in range(last):
                    ops[i // 2, t + 1, p] = op[slot, i, p, frame(slot, t), :]
                ops[i // 2, 0, p] = pltpu.roll(ops[i // 2, last, p], 1, 0)
                ops[i // 2, last + 1, p] = pltpu.roll(ops[i // 2, 1, p], 7, 0)

        def one(t, carry):
            def get(i, p):
                return op[slot, i, p, frame(slot, t), :]

            b0, b1 = OMEGA * get(1, 0), OMEGA * get(1, 1)
            v0, v1 = 0.5 * OMEGA * get(3, 0), 0.5 * OMEGA * get(3, 1)
            north = (b0, jnp.where(lane == 127, 0.0, b1))
            south = (jnp.where(lane == 0, 0.0, pltpu.roll(b1, 1, 1)), b0)
            v_north = (v1, jnp.where(lane == 127, 0.0, pltpu.roll(v0, 127, 1)))
            v_south = (jnp.where(lane == 0, 0.0, -pltpu.roll(v1, 1, 1)), -v0)
            for p in range(2):
                east, west = OMEGA * ops[0, t + 1, p], OMEGA * ops[0, t, p]
                co[slot, t, p, 0] = (1.0 - OMEGA) - (east + west + north[p] + south[p])
                co[slot, t, p, 1] = east
                co[slot, t, p, 2] = west
                co[slot, t, p, 3] = (south, north)[p][p]
                co[slot, t, p, 4] = (north, south)[p][p]
                co[slot, t, p, 5] = 0.5 * OMEGA * ops[1, t + 2, p]
                co[slot, t, p, 6] = -0.5 * OMEGA * ops[1, t, p]
                co[slot, t, p, 7] = (v_south, v_north)[p][p]
                co[slot, t, p, 8] = (v_north, v_south)[p][p]
            return carry

        lax.fori_loop(0, last, one, 0)

    def pads(slot, buf):
        for p in range(2):
            buf[0, p] = pltpu.roll(buf[TS[slot], p], 1, 1)
            buf[TS[slot] + 1, p] = pltpu.roll(buf[1, p], 7, 1)

    def store(dst, dst_n, t, p, value):
        dst[t + 1, p] = value
        dst_n[t + 1, 1 - p] = pltpu.roll(value, 1 if p else 127, 2)

    def sweep(slot, src, src_n, dst, dst_n, add):
        def one(t, carry):
            for p in range(2):
                diag = co[slot, t, p, 0]
                if add is None:
                    value = (diag + 1.0) * src[t + 1, p]
                else:
                    value = diag * src[t + 1, p] + add[t + 1, p]
                value = value + co[slot, t, p, 1] * src[t + 2, p] + co[slot, t, p, 2] * src[t, p]
                value = value + co[slot, t, p, 3] * src_n[t + 1, p] + co[slot, t, p, 4] * src[t + 1, 1 - p]
                store(dst, dst_n, t, p, value)
            return carry

        lax.fori_loop(0, TS[slot], one, 0, unroll=UNROLL)
        pads(slot, dst)

    def explicit_value(slot, k, t, p):
        value = fr[slot, k, :, p, frame(slot, t), :]
        value = value + co[slot, t, p, 5] * x2[t + 2, p] + co[slot, t, p, 6] * x2[t, p]
        value = value + co[slot, t, p, 7] * x2_n[t + 1, p] + co[slot, t, p, 8] * x2[t + 1, 1 - p]
        for g in range(F):
            value = value + mix[slot, g] * x2[t + 1, p, g]
        return value

    def step(slot, n):
        k = STEPS - 1 - n
        sweep(slot, r, r_n, x1, x1_n, None)
        sweep(slot, x1, x1_n, x2, x2_n, r)
        for c in range(STEPS):
            @pl.when((k == c) & (pair == 1))
            def _(c=c):
                wait_chunk(slot, c)

        return k

    def steps(slot, first):
        def one(n, carry):
            k = step(slot, n)

            def at(t, carry):
                for p in range(2):
                    store(r, r_n, t, p, explicit_value(slot, k, t, p))
                return carry

            lax.fori_loop(0, TS[slot], at, 0, unroll=UNROLL)
            pads(slot, r)
            return carry

        lax.fori_loop(first, STEPS - 1, one, 0)
        step(slot, STEPS - 1)
        for p in range(2):
            def at(t, carry, p=p):
                adj[1 - slot, :, p, adj_frame(slot, t), :] = explicit_value(slot, 0, t, p)
                return carry

            lax.fori_loop(0, TS[slot], at, 0, unroll=UNROLL)

            @pl.when(h == 1 - slot)
            def _(p=p):
                result_copy(1 - slot, p).start()

    def adj_frame(slot, t):
        return pl.ds(SIDE - WEST[slot] + t, 8, stride=TS[slot])

    def from_adj(slot):
        for t in range(TS[slot]):
            for p in range(2):
                store(r, r_n, t, p, adj[0, :, p, adj_frame(slot, t), :])
        pads(slot, r)

    def result_copy(phase, p):
        return pltpu.make_async_remote_copy(
            src_ref=adj.at[phase, :, p, pl.ds(SIDE, HALF)],
            dst_ref=res.at[:, p, pl.ds(pl.multiple_of(HALF * h, HALF), HALF)],
            send_sem=res_send.at[p], recv_sem=res_recv.at[p],
            device_id=partner, device_id_type=MESH,
        )

    def result_arrival(p):
        return pltpu.make_async_remote_copy(
            src_ref=adj.at[0, :, p, pl.ds(SIDE, HALF)],
            dst_ref=res.at[:, p, pl.ds(pl.multiple_of(HALF * o, HALF), HALF)],
            send_sem=res_send.at[p], recv_sem=res_recv.at[p],
            device_id=partner, device_id_type=MESH,
        )

    PIECES = [(inner, g) for inner in (True, False) for g in range(2)]

    def hand_main(n):
        inner, g = PIECES[n]
        ref = (pl.ds(F // 2 * g, F // 2), slice(None), pl.ds(pl.multiple_of(SIDE * (o if inner else h), SIDE), SIDE))
        return pltpu.make_async_remote_copy(
            src_ref=hand_out.at[ref], dst_ref=hand_in.at[ref], send_sem=hand_send.at[n], recv_sem=hand_recv.at[n],
            device_id=(h, space), device_id_type=MESH,
        )

    def hand_side():
        return pltpu.make_async_remote_copy(
            src_ref=side_out, dst_ref=side_in, send_sem=hand_send.at[4], recv_sem=hand_recv.at[4],
            device_id=(o, at_space(2 * h - 1)), device_id_type=MESH,
        )

    def relay(g):
        fields = pl.ds(F // 2 * g, F // 2)
        return pltpu.make_async_remote_copy(
            src_ref=hand_in.at[fields, :, pl.ds(pl.multiple_of(SIDE * o, SIDE), SIDE)], dst_ref=relay_in.at[fields],
            send_sem=hand_send.at[5 + g], recv_sem=hand_recv.at[5 + g],
            device_id=partner, device_id_type=MESH,
        )

    wait_chunk(1, OPS)
    coefficients(1)

    @pl.when(pair == 1)
    def _():
        wait_chunk(1, 3)
        for t in range(TS[1]):
            for p in range(2):
                store(r, r_n, t, p, fr[1, 3, :, p, frame(1, t), :])
        pads(1, r)

    @pl.when(pair == 0)
    def _():
        for c in range(STEPS):
            wait_chunk(1, c)
        wait_chunk(0, OPS)
        coefficients(0)
        for c in range(STEPS):
            wait_chunk(0, c)
        def take(fields, inner):
            rows = pl.multiple_of(SIDE * (o if inner else h), SIDE)
            adj[0, fields, :, pl.ds(SIDE + rows, SIDE)] = hand_in[fields, :, pl.ds(rows, SIDE)].astype(jnp.float32)

        for g in range(2):
            hand_main(g).wait_recv()
            relay(g).start()
            take(slice(F // 2 * g, F // 2 * (g + 1)), True)
        hand_side().wait_recv()
        both = side_in[...].astype(jnp.float32)
        for p in range(2):
            start = pl.multiple_of((SIDE - HALO) * o + (SIDE + HALF) * h, 8)
            adj[0, :, p, pl.ds(start, HALO)] = both[:, p * HALO:(p + 1) * HALO]
        for g in range(2):
            relay(g).wait_recv()
        adj[0, :, :, pl.ds(pl.multiple_of((SIDE + HALF) * o, SIDE), SIDE)] = relay_in[...].astype(jnp.float32)
        for g in range(2):
            hand_main(2 + g).wait_recv()
            take(slice(F // 2 * g, F // 2 * (g + 1)), False)
        from_adj(1)

    steps(1, pair)

    @pl.when(pair == 1)
    def _():
        wait_chunk(0, OPS)
        coefficients(0)

    from_adj(0)
    steps(0, 0)

    @pl.when(pair == 1)
    def _():
        start = pl.multiple_of(SIDE + (HALF - HALO) * h, 8)
        both = jnp.concatenate([adj[1, :, p, pl.ds(start, HALO)] for p in range(2)], axis=1)
        side_out[...] = both.astype(jnp.bfloat16)
        hand_side().start()
        for g in range(2):
            fields = slice(F // 2 * g, F // 2 * (g + 1))
            hand_out[fields] = adj[1, fields, :, SIDE:SIDE + HALF].astype(jnp.bfloat16)
            hand_main(g).start()
        for g in range(2):
            hand_main(2 + g).start()

    def out_copy(f):
        return pltpu.make_async_copy(outv.at[f], out.at[0, f], out_sem.at[f])

    own = adj.at[1 - h]
    res[:, :, pl.ds(pl.multiple_of(HALF * h, HALF), HALF)] = own[:, :, SIDE:SIDE + HALF]
    result_arrival(0).wait_recv()
    for f in range(F):
        outv[f, pl.ds(0, 128, stride=2), :] = jnp.transpose(res[f, 0])
    result_arrival(1).wait_recv()
    for f in range(F):
        outv[f, pl.ds(1, 128, stride=2), :] = jnp.transpose(res[f, 1])
        out_copy(f).start()

    for c in range(STEPS + 1):
        partner_copy(c).wait_send()
    for slot, left in ((0, (OPS, 3, 2, 1)), (1, (OPS, 3, 2, 1, 0))):
        @pl.when(h == slot)
        def _(slot=slot, left=left):
            for c in left:
                ext_sent(slot, c)

    cp_copy(h).wait_send()
    for p in range(2):
        result_copy(0, p).wait_send()

    @pl.when(pair == 1)
    def _():
        hand_side().wait_send()
        for n in range(4):
            hand_main(n).wait_send()

    @pl.when(pair == 0)
    def _():
        for g in range(2):
            relay(g).wait_send()

    for f in range(F):
        out_copy(f).wait()


def per_device(forcing, zonal_courant, meridional_courant, zonal_faces, meridional_faces, coupling):
    f32, bf16 = jnp.float32, jnp.bfloat16
    dma = pltpu.SemaphoreType.DMA
    state = pltpu.VMEM((T + 2, 2, F, 8, 128), f32)
    beside = pltpu.VMEM((T + 1, 2, F, 8, 128), f32)
    return pl.pallas_call(
        body,
        out_shape=jax.ShapeDtypeStruct((1,) + forcing.shape[2:], f32),
        in_specs=[pl.BlockSpec(memory_space=pl.ANY)] * 6,
        out_specs=pl.BlockSpec(memory_space=pl.ANY),
        scratch_shapes=[
            pltpu.VMEM((STEPS, F, 256, 128), bf16),
            pltpu.VMEM((4, 256, 128), f32),
            pltpu.VMEM((256, 128), f32),
            pltpu.VMEM((2, STEPS, F, 2, ROWS, 128), f32),
            pltpu.VMEM((2, 4, 2, ROWS, 128), f32),
            pltpu.VMEM((2, F, 1, F), f32),
            pltpu.VMEM((2, T + 2, 2, 8, 128), f32),
            pltpu.VMEM((2, STEPS + 1, F, 2 * HALO, 128), bf16),
            pltpu.VMEM((2, STEPS + 1, F, 2 * HALO, 128), bf16),
            pltpu.VMEM((2, T, 2, 9, 8, 128), f32),
            pltpu.VMEM((2, F, F, 8, 128), f32),
            state, state, state, beside, beside, beside,
            pltpu.VMEM((2, F, 2, HALF + 2 * SIDE, 128), f32),
            pltpu.VMEM((F, 2, HALF, 128), bf16),
            pltpu.VMEM((F, 2, HALF, 128), bf16),
            pltpu.VMEM((F, 2 * HALO, 128), bf16),
            pltpu.VMEM((F, 2 * HALO, 128), bf16),
            pltpu.VMEM((F, 2, SIDE, 128), bf16),
            pltpu.VMEM((F, 2, WIDTH, 128), f32),
            pltpu.VMEM((F, 256, 128), f32),
            dma((9,)), dma((F,)),
            dma((6,)), dma((6,)),
            dma((2, 5)), dma((2, 5)),
            dma((7,)), dma((7,)),
            dma((2,)), dma((2,)),
        ],
        compiler_params=pltpu.CompilerParams(
            collective_id=0, has_side_effects=True, vmem_limit_bytes=60 * 1024 * 1024
        ),
        name="adjoint_window",
    )(forcing, zonal_courant, meridional_courant, zonal_faces, meridional_faces, jnp.transpose(coupling, (1, 0, 2)))


def solution(mesh):
    return jax.shard_map(
        per_device,
        mesh=mesh,
        in_specs=(
            P("tm", None, None, None, "space"),
            P("tm", None, "space"),
            P("tm", None, "space"),
            P("tm", None, "space"),
            P("tm", None, "space"),
            P("tm", None, None),
        ),
        out_specs=P("tm", None, None, "space"),
        check_vma=False,
    )
```

```python
import jax
import jax.numpy as jnp
from jax import lax
from jax.experimental import pallas as pl
from jax.experimental.pallas import tpu as pltpu
from jax.sharding import PartitionSpec as P

OMEGA = 0.4
STEPS = 4
F = 6
WIDTH = 128
HALF = 64
HALO = 24
SIDE = 32
TS = (11, 14)
T = max(TS)
WEST = (12, 24)
ROWS = WIDTH + 2 * HALO
OPS = STEPS
EXT = ((0, 8, 8, 16, 16), (16, 16, 24, 24, 24))
MESH = pl.DeviceIdType.MESH
UNROLL = True


def body(
    forcing, courant_x, courant_y, faces_x, faces_y, coupling, out,
    nat_f, nat_o, even_odd, fr, op, cp, ops, ext_out, ext_in,
    co, mix, r, x1, x2, flux, r_n, x1_n, x2_n, adj, hand_out, hand_in, side_out, side_in, relay_in, res, outv,
    load_sem, out_sem, part_send, part_recv, ext_send, ext_recv,
    hand_send, hand_recv, res_send, res_recv,
):
    tm = lax.axis_index("tm")
    space = lax.axis_index("space")
    n_space = lax.axis_size("space")
    h = lax.rem(tm, 2)
    o = 1 - h
    pair = tm // 2

    def at_space(d):
        return lax.rem(space + d + n_space, n_space)

    barrier = pltpu.get_barrier_semaphore()
    count = 0
    for d in (-1, 1, 0):
        for j in range(4):
            if d == 0 and j == 0:
                continue
            other = lax.rem(tm + j, 4)
            pl.semaphore_signal(barrier, inc=1, device_id=(other, at_space(d)), device_id_type=MESH)
            count += 1

    ops_in = (faces_x, faces_y, courant_x, courant_y)
    loads = [pltpu.make_async_copy(ops_in[i].at[0], nat_o.at[i], load_sem.at[i]) for i in range(4)]
    loads.append(pltpu.make_async_copy(coupling, cp.at[h], load_sem.at[4]))
    loads += [pltpu.make_async_copy(forcing.at[0, k], nat_f.at[k], load_sem.at[5 + k]) for k in range(STEPS)]
    for i in (0, 1, 2, 3, 8, 4, 7, 6, 5):
        loads[i].start()

    partner = (2 * pair + o, space)
    to_east = (2 * pair, at_space(1))
    to_west = (2 * pair + 1, at_space(-1))

    def chunk(slot, c):
        return op.at[slot] if c == OPS else fr.at[slot, c]

    def partner_copy(c):
        ref = chunk(h, c).at[:, :, pl.ds(pl.multiple_of(HALO + 40 * o, 8), 88)]
        return pltpu.make_async_remote_copy(
            src_ref=ref, dst_ref=ref, send_sem=part_send.at[c], recv_sem=part_recv.at[c],
            device_id=partner, device_id_type=MESH,
        )

    def partner_arrival(c):
        ref = chunk(o, c).at[:, :, pl.ds(pl.multiple_of(HALO + 40 * h, 8), 88)]
        return pltpu.make_async_remote_copy(
            src_ref=ref, dst_ref=ref, send_sem=part_send.at[c], recv_sem=part_recv.at[c],
            device_id=partner, device_id_type=MESH,
        )

    def ext_pack(slot, c):
        n, ref = EXT[slot][c], chunk(slot, c)
        if n:
            for side in range(2):
                start = (HALO + WIDTH - n, HALO)[side]
                both = jnp.concatenate([ref[:, p, start:start + n] for p in range(2)], axis=1)
                ext_out[side, c, 0:both.shape[0], 0:2 * n] = both.astype(jnp.bfloat16)

    def ext_copies(slot, c):
        n, count = EXT[slot][c], chunk(slot, c).shape[0]
        if n == 0:
            return []
        return [
            pltpu.make_async_remote_copy(
                src_ref=ext_out.at[side, c, pl.ds(0, count), pl.ds(0, 2 * n)],
                dst_ref=ext_in.at[slot, c, pl.ds(0, count), pl.ds(0, 2 * n)],
                send_sem=ext_send.at[side, c], recv_sem=ext_recv.at[slot, c],
                device_id=(to_east, to_west)[side], device_id_type=MESH,
            )
            for side in range(2)
        ]

    def ext_start(slot, c):
        for copy in ext_copies(slot, c):
            copy.start()

    def ext_sent(slot, c):
        for copy in ext_copies(slot, c):
            copy.wait_send()

    def ext_arrival(slot, c):
        n, dest = EXT[slot][c], chunk(slot, c)
        ref = ext_in.at[slot, c, pl.ds(0, dest.shape[0]), pl.ds(0, 2 * n)]
        pltpu.make_async_remote_copy(
            src_ref=ref, dst_ref=ref, send_sem=ext_send.at[0, c], recv_sem=ext_recv.at[slot, c],
            device_id=to_east, device_id_type=MESH,
        ).wait_recv()
        start = pl.multiple_of((HALO - n) * o + (HALO + WIDTH) * h, 8)
        both = ext_in[slot, c, 0:dest.shape[0], 0:2 * n].astype(jnp.float32)
        for p in range(2):
            dest[:, p, pl.ds(start, n)] = both[:, p * n:(p + 1) * n]

    def wait_chunk(slot, c):
        @pl.when(h != slot)
        def _():
            partner_arrival(c).wait_recv()

        if EXT[slot][c]:
            ext_arrival(slot, c)

    def cp_copy(slot):
        return pltpu.make_async_remote_copy(
            src_ref=cp.at[slot], dst_ref=cp.at[slot],
            send_sem=part_send.at[5], recv_sem=part_recv.at[5],
            device_id=partner, device_id_type=MESH,
        )

    for slot in range(2):
        for c in range(STEPS + 1):
            n = EXT[slot][c]
            if n < HALO:
                ref = chunk(slot, c)
                start = pl.multiple_of((HALO + WIDTH + n) * h, 8)
                ref[:, :, pl.ds(start, HALO - n)] = jnp.zeros(ref.shape[:2] + (HALO - n, 128), jnp.float32)

    for i in range(4):
        loads[i].wait()
    for i in range(4):
        for p in range(2):
            op[h, i, p, HALO:HALO + WIDTH] = jnp.transpose(nat_o[i, pl.ds(p, 128, stride=2), :])
    def send_chunk(c):
        partner_copy(c).start()
        for slot in range(2):
            @pl.when(h == slot)
            def _(slot=slot):
                ext_pack(slot, c)
                if slot == 1:
                    ext_start(slot, c)

    early = lax.rem(space, 16) == 0

    @pl.when(jnp.logical_not(early))
    def _():
        pl.semaphore_wait(barrier, count)
        send_chunk(OPS)

    for k in (3, 2, 1, 0):
        loads[5 + k].wait()

        def one(f, carry, k=k):
            even_odd[...] = nat_f[k, f].astype(jnp.float32)
            for p in range(2):
                fr[h, k, f, p, HALO:HALO + WIDTH] = jnp.transpose(even_odd[pl.ds(p, 128, stride=2), :])
            return carry

        lax.fori_loop(0, F, one, 0)

        @pl.when(jnp.logical_not(early))
        def _(k=k):
            send_chunk(k)

    @pl.when(early)
    def _():
        pl.semaphore_wait(barrier, count)
        for c in (OPS, 3, 2, 1, 0):
            send_chunk(c)

    loads[4].wait()
    cp_copy(h).start()

    @pl.when(h == 0)
    def _():
        for c in (OPS, 3, 2, 1, 0):
            ext_start(0, c)

    lane = lax.broadcasted_iota(jnp.int32, (8, 128), 1)

    def frame(slot, t):
        return pl.ds(HALF * h + HALO - WEST[slot] + t, 8, stride=TS[slot])

    def coefficients(slot):
        @pl.when(h != slot)
        def _():
            cp_copy(o).wait_recv()

        last = TS[slot]
        for g in range(F):
            row = cp[slot, g]
            for f in range(F):
                value = jnp.broadcast_to(row[:, f:f + 1], (8, 128))
                mix[slot, g, f] = OMEGA * (value + 1.0) if g == f else OMEGA * value

        for p in range(2):
            for t in range(last):
                ops[t + 1, p] = op[slot, 0, p, frame(slot, t), :]
            ops[0, p] = pltpu.roll(ops[last, p], 1, 0)

        def one(t, carry):
            def get(i, p):
                return op[slot, i, p, frame(slot, t), :]

            b0, b1 = OMEGA * get(1, 0), OMEGA * get(1, 1)
            v0, v1 = 0.5 * OMEGA * get(3, 0), 0.5 * OMEGA * get(3, 1)
            north = (b0, jnp.where(lane == 127, 0.0, b1))
            south = (jnp.where(lane == 0, 0.0, pltpu.roll(b1, 1, 1)), b0)
            v_north = (v1, jnp.where(lane == 127, 0.0, pltpu.roll(v0, 127, 1)))
            v_south = (jnp.where(lane == 0, 0.0, -pltpu.roll(v1, 1, 1)), -v0)
            for p in range(2):
                east, west = OMEGA * ops[t + 1, p], OMEGA * ops[t, p]
                co[slot, t, p, 0] = (1.0 - OMEGA) - (east + west + north[p] + south[p])
                co[slot, t, p, 1] = east
                co[slot, t, p, 2] = west
                co[slot, t, p, 3] = (south, north)[p][p]
                co[slot, t, p, 4] = (north, south)[p][p]
                co[slot, t, p, 5] = 0.5 * OMEGA * get(2, p)
                co[slot, t, p, 6] = (v_south, v_north)[p][p]
                co[slot, t, p, 7] = (v_north, v_south)[p][p]
            return carry

        lax.fori_loop(0, last, one, 0)

    def pads(slot, buf):
        for p in range(2):
            buf[0, p] = pltpu.roll(buf[TS[slot], p], 1, 1)
            buf[TS[slot] + 1, p] = pltpu.roll(buf[1, p], 7, 1)

    def store(dst, dst_n, t, p, value):
        dst[t + 1, p] = value
        dst_n[t + 1, 1 - p] = pltpu.roll(value, 1 if p else 127, 2)

    def sweep(slot, src, src_n, dst, dst_n, add):
        def one(t, carry):
            for p in range(2):
                diag = co[slot, t, p, 0]
                if add is None:
                    value = (diag + 1.0) * src[t + 1, p]
                else:
                    value = diag * src[t + 1, p] + add[t + 1, p]
                value = value + co[slot, t, p, 1] * src[t + 2, p] + co[slot, t, p, 2] * src[t, p]
                value = value + co[slot, t, p, 3] * src_n[t + 1, p] + co[slot, t, p, 4] * src[t + 1, 1 - p]
                store(dst, dst_n, t, p, value)
                if add is not None:
                    flux[t + 1, p] = co[slot, t, p, 5] * value
            return carry

        lax.fori_loop(0, TS[slot], one, 0, unroll=UNROLL)
        pads(slot, dst if add is None else flux)

    def explicit_value(slot, k, t, p):
        value = fr[slot, k, :, p, frame(slot, t), :]
        value = value + flux[t + 2, p] - flux[t, p]
        value = value + co[slot, t, p, 6] * x2_n[t + 1, p] + co[slot, t, p, 7] * x2[t + 1, 1 - p]
        for g in range(F):
            value = value + mix[slot, g] * x2[t + 1, p, g]
        return value

    def step(slot, n):
        k = STEPS - 1 - n
        sweep(slot, r, r_n, x1, x1_n, None)
        sweep(slot, x1, x1_n, x2, x2_n, r)
        for c in range(STEPS):
            @pl.when((k == c) & (pair == 1))
            def _(c=c):
                wait_chunk(slot, c)

        return k

    def steps(slot, first):
        def one(n, carry):
            k = step(slot, n)

            def at(t, carry):
                for p in range(2):
                    store(r, r_n, t, p, explicit_value(slot, k, t, p))
                return carry

            lax.fori_loop(0, TS[slot], at, 0, unroll=UNROLL)
            pads(slot, r)
            return carry

        lax.fori_loop(first, STEPS - 1, one, 0)
        step(slot, STEPS - 1)
        for p in range(2):
            def at(t, carry, p=p):
                adj[1 - slot, :, p, adj_frame(slot, t), :] = explicit_value(slot, 0, t, p)
                return carry

            lax.fori_loop(0, TS[slot], at, 0, unroll=UNROLL)

            @pl.when(h == 1 - slot)
            def _(p=p):
                result_copy(1 - slot, p).start()

    def adj_frame(slot, t):
        return pl.ds(SIDE - WEST[slot] + t, 8, stride=TS[slot])

    def from_adj(slot):
        for t in range(TS[slot]):
            for p in range(2):
                store(r, r_n, t, p, adj[0, :, p, adj_frame(slot, t), :])
        pads(slot, r)

    def result_copy(phase, p):
        return pltpu.make_async_remote_copy(
            src_ref=adj.at[phase, :, p, pl.ds(SIDE, HALF)],
            dst_ref=res.at[:, p, pl.ds(pl.multiple_of(HALF * h, HALF), HALF)],
            send_sem=res_send.at[p], recv_sem=res_recv.at[p],
            device_id=partner, device_id_type=MESH,
        )

    def result_arrival(p):
        return pltpu.make_async_remote_copy(
            src_ref=adj.at[0, :, p, pl.ds(SIDE, HALF)],
            dst_ref=res.at[:, p, pl.ds(pl.multiple_of(HALF * o, HALF), HALF)],
            send_sem=res_send.at[p], recv_sem=res_recv.at[p],
            device_id=partner, device_id_type=MESH,
        )

    PIECES = [(inner, g) for inner in (True, False) for g in range(2)]

    def hand_main(n):
        inner, g = PIECES[n]
        ref = (pl.ds(F // 2 * g, F // 2), slice(None), pl.ds(pl.multiple_of(SIDE * (o if inner else h), SIDE), SIDE))
        return pltpu.make_async_remote_copy(
            src_ref=hand_out.at[ref], dst_ref=hand_in.at[ref], send_sem=hand_send.at[n], recv_sem=hand_recv.at[n],
            device_id=(h, space), device_id_type=MESH,
        )

    def hand_side():
        return pltpu.make_async_remote_copy(
            src_ref=side_out, dst_ref=side_in, send_sem=hand_send.at[4], recv_sem=hand_recv.at[4],
            device_id=(o, at_space(2 * h - 1)), device_id_type=MESH,
        )

    def relay(g):
        fields = pl.ds(F // 2 * g, F // 2)
        return pltpu.make_async_remote_copy(
            src_ref=hand_in.at[fields, :, pl.ds(pl.multiple_of(SIDE * o, SIDE), SIDE)], dst_ref=relay_in.at[fields],
            send_sem=hand_send.at[5 + g], recv_sem=hand_recv.at[5 + g],
            device_id=partner, device_id_type=MESH,
        )

    wait_chunk(1, OPS)
    coefficients(1)

    @pl.when(pair == 1)
    def _():
        wait_chunk(1, 3)
        for t in range(TS[1]):
            for p in range(2):
                store(r, r_n, t, p, fr[1, 3, :, p, frame(1, t), :])
        pads(1, r)

    @pl.when(pair == 0)
    def _():
        for c in range(STEPS):
            wait_chunk(1, c)
        wait_chunk(0, OPS)
        coefficients(0)
        for c in range(STEPS):
            wait_chunk(0, c)
        def take(fields, inner):
            rows = pl.multiple_of(SIDE * (o if inner else h), SIDE)
            adj[0, fields, :, pl.ds(SIDE + rows, SIDE)] = hand_in[fields, :, pl.ds(rows, SIDE)].astype(jnp.float32)

        for g in range(2):
            hand_main(g).wait_recv()
            relay(g).start()
            take(slice(F // 2 * g, F // 2 * (g + 1)), True)
        hand_side().wait_recv()
        both = side_in[...].astype(jnp.float32)
        for p in range(2):
            start = pl.multiple_of((SIDE - HALO) * o + (SIDE + HALF) * h, 8)
            adj[0, :, p, pl.ds(start, HALO)] = both[:, p * HALO:(p + 1) * HALO]
        for g in range(2):
            relay(g).wait_recv()
        adj[0, :, :, pl.ds(pl.multiple_of((SIDE + HALF) * o, SIDE), SIDE)] = relay_in[...].astype(jnp.float32)
        for g in range(2):
            hand_main(2 + g).wait_recv()
            take(slice(F // 2 * g, F // 2 * (g + 1)), False)
        from_adj(1)

    steps(1, pair)

    @pl.when(pair == 1)
    def _():
        wait_chunk(0, OPS)
        coefficients(0)

    from_adj(0)
    steps(0, 0)

    @pl.when(pair == 1)
    def _():
        start = pl.multiple_of(SIDE + (HALF - HALO) * h, 8)
        both = jnp.concatenate([adj[1, :, p, pl.ds(start, HALO)] for p in range(2)], axis=1)
        side_out[...] = both.astype(jnp.bfloat16)
        hand_side().start()
        for g in range(2):
            fields = slice(F // 2 * g, F // 2 * (g + 1))
            hand_out[fields] = adj[1, fields, :, SIDE:SIDE + HALF].astype(jnp.bfloat16)
            hand_main(g).start()
        for g in range(2):
            hand_main(2 + g).start()

    def out_copy(f):
        return pltpu.make_async_copy(outv.at[f], out.at[0, f], out_sem.at[f])

    own = adj.at[1 - h]
    res[:, :, pl.ds(pl.multiple_of(HALF * h, HALF), HALF)] = own[:, :, SIDE:SIDE + HALF]
    result_arrival(0).wait_recv()
    for f in range(F):
        outv[f, pl.ds(0, 128, stride=2), :] = jnp.transpose(res[f, 0])
    result_arrival(1).wait_recv()
    for f in range(F):
        outv[f, pl.ds(1, 128, stride=2), :] = jnp.transpose(res[f, 1])
        out_copy(f).start()

    for c in range(STEPS + 1):
        partner_copy(c).wait_send()
    for slot, left in ((0, (OPS, 3, 2, 1)), (1, (OPS, 3, 2, 1, 0))):
        @pl.when(h == slot)
        def _(slot=slot, left=left):
            for c in left:
                ext_sent(slot, c)

    cp_copy(h).wait_send()
    for p in range(2):
        result_copy(0, p).wait_send()

    @pl.when(pair == 1)
    def _():
        hand_side().wait_send()
        for n in range(4):
            hand_main(n).wait_send()

    @pl.when(pair == 0)
    def _():
        for g in range(2):
            relay(g).wait_send()

    for f in range(F):
        out_copy(f).wait()


def per_device(forcing, zonal_courant, meridional_courant, zonal_faces, meridional_faces, coupling):
    f32, bf16 = jnp.float32, jnp.bfloat16
    dma = pltpu.SemaphoreType.DMA
    state = pltpu.VMEM((T + 2, 2, F, 8, 128), f32)
    beside = pltpu.VMEM((T + 1, 2, F, 8, 128), f32)
    return pl.pallas_call(
        body,
        out_shape=jax.ShapeDtypeStruct((1,) + forcing.shape[2:], f32),
        in_specs=[pl.BlockSpec(memory_space=pl.ANY)] * 6,
        out_specs=pl.BlockSpec(memory_space=pl.ANY),
        scratch_shapes=[
            pltpu.VMEM((STEPS, F, 256, 128), bf16),
            pltpu.VMEM((4, 256, 128), f32),
            pltpu.VMEM((256, 128), f32),
            pltpu.VMEM((2, STEPS, F, 2, ROWS, 128), f32),
            pltpu.VMEM((2, 4, 2, ROWS, 128), f32),
            pltpu.VMEM((2, F, 1, F), f32),
            pltpu.VMEM((T + 1, 2, 8, 128), f32),
            pltpu.VMEM((2, STEPS + 1, F, 2 * HALO, 128), bf16),
            pltpu.VMEM((2, STEPS + 1, F, 2 * HALO, 128), bf16),
            pltpu.VMEM((2, T, 2, 8, 8, 128), f32),
            pltpu.VMEM((2, F, F, 8, 128), f32),
            state, state, state, state, beside, beside, beside,
            pltpu.VMEM((2, F, 2, HALF + 2 * SIDE, 128), f32),
            pltpu.VMEM((F, 2, HALF, 128), bf16),
            pltpu.VMEM((F, 2, HALF, 128), bf16),
            pltpu.VMEM((F, 2 * HALO, 128), bf16),
            pltpu.VMEM((F, 2 * HALO, 128), bf16),
            pltpu.VMEM((F, 2, SIDE, 128), bf16),
            pltpu.VMEM((F, 2, WIDTH, 128), f32),
            pltpu.VMEM((F, 256, 128), f32),
            dma((9,)), dma((F,)),
            dma((6,)), dma((6,)),
            dma((2, 5)), dma((2, 5)),
            dma((7,)), dma((7,)),
            dma((2,)), dma((2,)),
        ],
        compiler_params=pltpu.CompilerParams(
            collective_id=0, has_side_effects=True, vmem_limit_bytes=60 * 1024 * 1024
        ),
        name="adjoint_window",
    )(forcing, zonal_courant, meridional_courant, zonal_faces, meridional_faces, jnp.transpose(coupling, (1, 0, 2)))


def solution(mesh):
    return jax.shard_map(
        per_device,
        mesh=mesh,
        in_specs=(
            P("tm", None, None, None, "space"),
            P("tm", None, "space"),
            P("tm", None, "space"),
            P("tm", None, "space"),
            P("tm", None, "space"),
            P("tm", None, None),
        ),
        out_specs=P("tm", None, None, "space"),
        check_vma=False,
    )
```

```python
import jax
import jax.numpy as jnp
from jax import lax
from jax.experimental import pallas as pl
from jax.experimental.pallas import tpu as pltpu
from jax.sharding import PartitionSpec as P

OMEGA = 0.4
STEPS = 4
F = 6
WIDTH = 128
HALF = 64
HALO = 24
SIDE = 32
TS = (11, 14)
T = max(TS)
WEST = (12, 24)
ROWS = WIDTH + 2 * HALO
OPS = STEPS
EXT = ((0, 8, 8, 16, 16), (16, 16, 24, 24, 24))
MESH = pl.DeviceIdType.MESH
UNROLL = True


def body(
    forcing, courant_x, courant_y, faces_x, faces_y, coupling, out,
    nat_f, nat_o, even_odd, fr, op, cp, ops, ext_out, ext_in,
    co, mix, r, x1, x2, flux, r_n, x1_n, x2_n, adj, hand_out, hand_in, side_out, side_in, relay_in, res, outv,
    load_sem, out_sem, part_send, part_recv, ext_send, ext_recv,
    hand_send, hand_recv, res_send, res_recv,
):
    tm = lax.axis_index("tm")
    space = lax.axis_index("space")
    n_space = lax.axis_size("space")
    h = lax.rem(tm, 2)
    o = 1 - h
    pair = tm // 2

    def at_space(d):
        return lax.rem(space + d + n_space, n_space)

    barrier = pltpu.get_barrier_semaphore()
    count = 0
    for d in (-1, 1, 0):
        for j in range(4):
            if d == 0 and j == 0:
                continue
            other = lax.rem(tm + j, 4)
            pl.semaphore_signal(barrier, inc=1, device_id=(other, at_space(d)), device_id_type=MESH)
            count += 1

    ops_in = (faces_x, faces_y, courant_x, courant_y)
    loads = [pltpu.make_async_copy(ops_in[i].at[0], nat_o.at[i], load_sem.at[i]) for i in range(4)]
    loads.append(pltpu.make_async_copy(coupling, cp.at[h], load_sem.at[4]))
    loads += [pltpu.make_async_copy(forcing.at[0, k], nat_f.at[k], load_sem.at[5 + k]) for k in range(STEPS)]
    for i in (0, 1, 2, 3, 8):
        loads[i].start()

    partner = (2 * pair + o, space)
    to_east = (2 * pair, at_space(1))
    to_west = (2 * pair + 1, at_space(-1))

    def chunk(slot, c):
        return op.at[slot] if c == OPS else fr.at[slot, c]

    def partner_copy(c):
        ref = chunk(h, c).at[:, :, pl.ds(pl.multiple_of(HALO + 40 * o, 8), 88)]
        return pltpu.make_async_remote_copy(
            src_ref=ref, dst_ref=ref, send_sem=part_send.at[c], recv_sem=part_recv.at[c],
            device_id=partner, device_id_type=MESH,
        )

    def partner_arrival(c):
        ref = chunk(o, c).at[:, :, pl.ds(pl.multiple_of(HALO + 40 * h, 8), 88)]
        return pltpu.make_async_remote_copy(
            src_ref=ref, dst_ref=ref, send_sem=part_send.at[c], recv_sem=part_recv.at[c],
            device_id=partner, device_id_type=MESH,
        )

    def ext_pack(slot, c):
        n, ref = EXT[slot][c], chunk(slot, c)
        if n:
            for side in range(2):
                start = (HALO + WIDTH - n, HALO)[side]
                both = jnp.concatenate([ref[:, p, start:start + n] for p in range(2)], axis=1)
                ext_out[side, c, 0:both.shape[0], 0:2 * n] = both.astype(jnp.bfloat16)

    def ext_copies(slot, c):
        n, count = EXT[slot][c], chunk(slot, c).shape[0]
        if n == 0:
            return []
        return [
            pltpu.make_async_remote_copy(
                src_ref=ext_out.at[side, c, pl.ds(0, count), pl.ds(0, 2 * n)],
                dst_ref=ext_in.at[slot, c, pl.ds(0, count), pl.ds(0, 2 * n)],
                send_sem=ext_send.at[side, c], recv_sem=ext_recv.at[slot, c],
                device_id=(to_east, to_west)[side], device_id_type=MESH,
            )
            for side in range(2)
        ]

    def ext_start(slot, c):
        for copy in ext_copies(slot, c):
            copy.start()

    def ext_sent(slot, c):
        for copy in ext_copies(slot, c):
            copy.wait_send()

    def ext_arrival(slot, c):
        n, dest = EXT[slot][c], chunk(slot, c)
        ref = ext_in.at[slot, c, pl.ds(0, dest.shape[0]), pl.ds(0, 2 * n)]
        pltpu.make_async_remote_copy(
            src_ref=ref, dst_ref=ref, send_sem=ext_send.at[0, c], recv_sem=ext_recv.at[slot, c],
            device_id=to_east, device_id_type=MESH,
        ).wait_recv()
        start = pl.multiple_of((HALO - n) * o + (HALO + WIDTH) * h, 8)
        both = ext_in[slot, c, 0:dest.shape[0], 0:2 * n].astype(jnp.float32)
        for p in range(2):
            dest[:, p, pl.ds(start, n)] = both[:, p * n:(p + 1) * n]

    def wait_chunk(slot, c):
        @pl.when(h != slot)
        def _():
            partner_arrival(c).wait_recv()

        if EXT[slot][c]:
            ext_arrival(slot, c)

    def cp_copy(slot):
        return pltpu.make_async_remote_copy(
            src_ref=cp.at[slot], dst_ref=cp.at[slot],
            send_sem=part_send.at[5], recv_sem=part_recv.at[5],
            device_id=partner, device_id_type=MESH,
        )

    for slot in range(2):
        for c in range(STEPS + 1):
            n = EXT[slot][c]
            if n < HALO:
                ref = chunk(slot, c)
                start = pl.multiple_of((HALO + WIDTH + n) * h, 8)
                ref[:, :, pl.ds(start, HALO - n)] = jnp.zeros(ref.shape[:2] + (HALO - n, 128), jnp.float32)

    for i in range(4):
        loads[i].wait()
    for i in (4, 7, 6, 5):
        loads[i].start()
    for i in range(4):
        for p in range(2):
            op[h, i, p, HALO:HALO + WIDTH] = jnp.transpose(nat_o[i, pl.ds(p, 128, stride=2), :])
    def send_chunk(c):
        partner_copy(c).start()
        for slot in range(2):
            @pl.when(h == slot)
            def _(slot=slot):
                ext_pack(slot, c)
                if slot == 1:
                    ext_start(slot, c)

    early = lax.rem(space, 16) == 0

    @pl.when(jnp.logical_not(early))
    def _():
        pl.semaphore_wait(barrier, count)
        send_chunk(OPS)

    for k in (3, 2, 1, 0):
        loads[5 + k].wait()

        def one(f, carry, k=k):
            even_odd[...] = nat_f[k, f].astype(jnp.float32)
            for p in range(2):
                fr[h, k, f, p, HALO:HALO + WIDTH] = jnp.transpose(even_odd[pl.ds(p, 128, stride=2), :])
            return carry

        lax.fori_loop(0, F, one, 0)

        @pl.when(jnp.logical_not(early))
        def _(k=k):
            send_chunk(k)

    @pl.when(early)
    def _():
        pl.semaphore_wait(barrier, count)
        for c in (OPS, 3, 2, 1, 0):
            send_chunk(c)

    loads[4].wait()
    cp_copy(h).start()

    @pl.when(h == 0)
    def _():
        for c in (OPS, 3, 2, 1, 0):
            ext_start(0, c)

    lane = lax.broadcasted_iota(jnp.int32, (8, 128), 1)

    def frame(slot, t):
        return pl.ds(HALF * h + HALO - WEST[slot] + t, 8, stride=TS[slot])

    def coefficients(slot):
        @pl.when(h != slot)
        def _():
            cp_copy(o).wait_recv()

        last = TS[slot]
        for g in range(F):
            row = cp[slot, g]
            for f in range(F):
                value = jnp.broadcast_to(row[:, f:f + 1], (8, 128))
                mix[slot, g, f] = OMEGA * (value + 1.0) if g == f else OMEGA * value

        for p in range(2):
            for t in range(last):
                ops[t + 1, p] = op[slot, 0, p, frame(slot, t), :]
            ops[0, p] = pltpu.roll(ops[last, p], 1, 0)

        def one(t, carry):
            def get(i, p):
                return op[slot, i, p, frame(slot, t), :]

            b0, b1 = OMEGA * get(1, 0), OMEGA * get(1, 1)
            v0, v1 = 0.5 * OMEGA * get(3, 0), 0.5 * OMEGA * get(3, 1)
            north = (b0, jnp.where(lane == 127, 0.0, b1))
            south = (jnp.where(lane == 0, 0.0, pltpu.roll(b1, 1, 1)), b0)
            v_north = (v1, jnp.where(lane == 127, 0.0, pltpu.roll(v0, 127, 1)))
            v_south = (jnp.where(lane == 0, 0.0, -pltpu.roll(v1, 1, 1)), -v0)
            for p in range(2):
                east, west = OMEGA * ops[t + 1, p], OMEGA * ops[t, p]
                co[slot, t, p, 0] = (1.0 - OMEGA) - (east + west + north[p] + south[p])
                co[slot, t, p, 1] = east
                co[slot, t, p, 2] = west
                co[slot, t, p, 3] = (south, north)[p][p]
                co[slot, t, p, 4] = (north, south)[p][p]
                co[slot, t, p, 5] = 0.5 * OMEGA * get(2, p)
                co[slot, t, p, 6] = (v_south, v_north)[p][p]
                co[slot, t, p, 7] = (v_north, v_south)[p][p]
            return carry

        lax.fori_loop(0, last, one, 0)

    def pads(slot, buf):
        for p in range(2):
            buf[0, p] = pltpu.roll(buf[TS[slot], p], 1, 1)
            buf[TS[slot] + 1, p] = pltpu.roll(buf[1, p], 7, 1)

    def store(dst, dst_n, t, p, value):
        dst[t + 1, p] = value
        dst_n[t + 1, 1 - p] = pltpu.roll(value, 1 if p else 127, 2)

    def sweep(slot, src, src_n, dst, dst_n, add):
        def one(t, carry):
            for p in range(2):
                diag = co[slot, t, p, 0]
                if add is None:
                    value = (diag + 1.0) * src[t + 1, p]
                else:
                    value = diag * src[t + 1, p] + add[t + 1, p]
                value = value + co[slot, t, p, 1] * src[t + 2, p] + co[slot, t, p, 2] * src[t, p]
                value = value + co[slot, t, p, 3] * src_n[t + 1, p] + co[slot, t, p, 4] * src[t + 1, 1 - p]
                store(dst, dst_n, t, p, value)
                if add is not None:
                    flux[t + 1, p] = co[slot, t, p, 5] * value
            return carry

        lax.fori_loop(0, TS[slot], one, 0, unroll=UNROLL)
        pads(slot, dst if add is None else flux)

    def explicit_value(slot, k, t, p):
        value = fr[slot, k, :, p, frame(slot, t), :]
        value = value + flux[t + 2, p] - flux[t, p]
        value = value + co[slot, t, p, 6] * x2_n[t + 1, p] + co[slot, t, p, 7] * x2[t + 1, 1 - p]
        for g in range(F):
            value = value + mix[slot, g] * x2[t + 1, p, g]
        return value

    def step(slot, n):
        k = STEPS - 1 - n
        sweep(slot, r, r_n, x1, x1_n, None)
        sweep(slot, x1, x1_n, x2, x2_n, r)
        for c in range(STEPS):
            @pl.when((k == c) & (pair == 1))
            def _(c=c):
                wait_chunk(slot, c)

        return k

    def steps(slot, first):
        def one(n, carry):
            k = step(slot, n)

            def at(t, carry):
                for p in range(2):
                    store(r, r_n, t, p, explicit_value(slot, k, t, p))
                return carry

            lax.fori_loop(0, TS[slot], at, 0, unroll=UNROLL)
            pads(slot, r)
            return carry

        lax.fori_loop(first, STEPS - 1, one, 0)
        step(slot, STEPS - 1)
        for p in range(2):
            def at(t, carry, p=p):
                adj[1 - slot, :, p, adj_frame(slot, t), :] = explicit_value(slot, 0, t, p)
                return carry

            lax.fori_loop(0, TS[slot], at, 0, unroll=UNROLL)

            @pl.when(h == 1 - slot)
            def _(p=p):
                for n in ((0,), (1, 2))[p]:
                    result_copy(1 - slot, n).start()

    def adj_frame(slot, t):
        return pl.ds(SIDE - WEST[slot] + t, 8, stride=TS[slot])

    def from_adj(slot):
        for t in range(TS[slot]):
            for p in range(2):
                store(r, r_n, t, p, adj[0, :, p, adj_frame(slot, t), :])
        pads(slot, r)

    PARTS = [(0, slice(0, F)), (1, slice(0, F // 2)), (1, slice(F // 2, F))]

    def result_copy(phase, n):
        p, fields = PARTS[n]
        fields = pl.ds(fields.start, fields.stop - fields.start)
        return pltpu.make_async_remote_copy(
            src_ref=adj.at[phase, fields, p, pl.ds(SIDE, HALF)],
            dst_ref=res.at[fields, p, pl.ds(pl.multiple_of(HALF * h, HALF), HALF)],
            send_sem=res_send.at[n], recv_sem=res_recv.at[n],
            device_id=partner, device_id_type=MESH,
        )

    def result_arrival(n):
        p, fields = PARTS[n]
        fields = pl.ds(fields.start, fields.stop - fields.start)
        return pltpu.make_async_remote_copy(
            src_ref=adj.at[0, fields, p, pl.ds(SIDE, HALF)],
            dst_ref=res.at[fields, p, pl.ds(pl.multiple_of(HALF * o, HALF), HALF)],
            send_sem=res_send.at[n], recv_sem=res_recv.at[n],
            device_id=partner, device_id_type=MESH,
        )

    PIECES = [(inner, g) for inner in (True, False) for g in range(2)]

    def hand_main(n):
        inner, g = PIECES[n]
        ref = (pl.ds(F // 2 * g, F // 2), slice(None), pl.ds(pl.multiple_of(SIDE * (o if inner else h), SIDE), SIDE))
        return pltpu.make_async_remote_copy(
            src_ref=hand_out.at[ref], dst_ref=hand_in.at[ref], send_sem=hand_send.at[n], recv_sem=hand_recv.at[n],
            device_id=(h, space), device_id_type=MESH,
        )

    def hand_side():
        return pltpu.make_async_remote_copy(
            src_ref=side_out, dst_ref=side_in, send_sem=hand_send.at[4], recv_sem=hand_recv.at[4],
            device_id=(o, at_space(2 * h - 1)), device_id_type=MESH,
        )

    def relay(g):
        fields = pl.ds(F // 2 * g, F // 2)
        return pltpu.make_async_remote_copy(
            src_ref=hand_in.at[fields, :, pl.ds(pl.multiple_of(SIDE * o, SIDE), SIDE)], dst_ref=relay_in.at[fields],
            send_sem=hand_send.at[5 + g], recv_sem=hand_recv.at[5 + g],
            device_id=partner, device_id_type=MESH,
        )

    wait_chunk(1, OPS)
    coefficients(1)

    @pl.when(pair == 1)
    def _():
        wait_chunk(1, 3)
        for t in range(TS[1]):
            for p in range(2):
                store(r, r_n, t, p, fr[1, 3, :, p, frame(1, t), :])
        pads(1, r)

    @pl.when(pair == 0)
    def _():
        for c in range(STEPS):
            wait_chunk(1, c)
        wait_chunk(0, OPS)
        coefficients(0)
        for c in range(STEPS):
            wait_chunk(0, c)
        def take(fields, inner):
            rows = pl.multiple_of(SIDE * (o if inner else h), SIDE)
            adj[0, fields, :, pl.ds(SIDE + rows, SIDE)] = hand_in[fields, :, pl.ds(rows, SIDE)].astype(jnp.float32)

        for g in range(2):
            hand_main(g).wait_recv()
            relay(g).start()
            take(slice(F // 2 * g, F // 2 * (g + 1)), True)
        hand_side().wait_recv()
        both = side_in[...].astype(jnp.float32)
        for p in range(2):
            start = pl.multiple_of((SIDE - HALO) * o + (SIDE + HALF) * h, 8)
            adj[0, :, p, pl.ds(start, HALO)] = both[:, p * HALO:(p + 1) * HALO]
        for g in range(2):
            relay(g).wait_recv()
        adj[0, :, :, pl.ds(pl.multiple_of((SIDE + HALF) * o, SIDE), SIDE)] = relay_in[...].astype(jnp.float32)
        for g in range(2):
            hand_main(2 + g).wait_recv()
            take(slice(F // 2 * g, F // 2 * (g + 1)), False)
        from_adj(1)

    steps(1, pair)

    @pl.when(pair == 1)
    def _():
        wait_chunk(0, OPS)
        coefficients(0)

    from_adj(0)
    steps(0, 0)

    @pl.when(pair == 1)
    def _():
        start = pl.multiple_of(SIDE + (HALF - HALO) * h, 8)
        both = jnp.concatenate([adj[1, :, p, pl.ds(start, HALO)] for p in range(2)], axis=1)
        side_out[...] = both.astype(jnp.bfloat16)
        hand_side().start()
        for g in range(2):
            fields = slice(F // 2 * g, F // 2 * (g + 1))
            hand_out[fields] = adj[1, fields, :, SIDE:SIDE + HALF].astype(jnp.bfloat16)
            hand_main(g).start()
        for g in range(2):
            hand_main(2 + g).start()

    def out_copy(f):
        return pltpu.make_async_copy(outv.at[f], out.at[0, f], out_sem.at[f])

    own = adj.at[1 - h]
    res[:, :, pl.ds(pl.multiple_of(HALF * h, HALF), HALF)] = own[:, :, SIDE:SIDE + HALF]
    for n in range(3):
        result_arrival(n).wait_recv()
        p, fields = PARTS[n]
        for f in range(fields.start, fields.stop):
            outv[f, pl.ds(p, 128, stride=2), :] = jnp.transpose(res[f, p])
            if p == 1:
                out_copy(f).start()

    for c in range(STEPS + 1):
        partner_copy(c).wait_send()
    for slot, left in ((0, (OPS, 3, 2, 1)), (1, (OPS, 3, 2, 1, 0))):
        @pl.when(h == slot)
        def _(slot=slot, left=left):
            for c in left:
                ext_sent(slot, c)

    cp_copy(h).wait_send()
    for n in range(3):
        result_copy(0, n).wait_send()

    @pl.when(pair == 1)
    def _():
        hand_side().wait_send()
        for n in range(4):
            hand_main(n).wait_send()

    @pl.when(pair == 0)
    def _():
        for g in range(2):
            relay(g).wait_send()

    for f in range(F):
        out_copy(f).wait()


def per_device(forcing, zonal_courant, meridional_courant, zonal_faces, meridional_faces, coupling):
    f32, bf16 = jnp.float32, jnp.bfloat16
    dma = pltpu.SemaphoreType.DMA
    state = pltpu.VMEM((T + 2, 2, F, 8, 128), f32)
    beside = pltpu.VMEM((T + 1, 2, F, 8, 128), f32)
    return pl.pallas_call(
        body,
        out_shape=jax.ShapeDtypeStruct((1,) + forcing.shape[2:], f32),
        in_specs=[pl.BlockSpec(memory_space=pl.ANY)] * 6,
        out_specs=pl.BlockSpec(memory_space=pl.ANY),
        scratch_shapes=[
            pltpu.VMEM((STEPS, F, 256, 128), bf16),
            pltpu.VMEM((4, 256, 128), f32),
            pltpu.VMEM((256, 128), f32),
            pltpu.VMEM((2, STEPS, F, 2, ROWS, 128), f32),
            pltpu.VMEM((2, 4, 2, ROWS, 128), f32),
            pltpu.VMEM((2, F, 1, F), f32),
            pltpu.VMEM((T + 1, 2, 8, 128), f32),
            pltpu.VMEM((2, STEPS + 1, F, 2 * HALO, 128), bf16),
            pltpu.VMEM((2, STEPS + 1, F, 2 * HALO, 128), bf16),
            pltpu.VMEM((2, T, 2, 8, 8, 128), f32),
            pltpu.VMEM((2, F, F, 8, 128), f32),
            state, state, state, state, beside, beside, beside,
            pltpu.VMEM((2, F, 2, HALF + 2 * SIDE, 128), f32),
            pltpu.VMEM((F, 2, HALF, 128), bf16),
            pltpu.VMEM((F, 2, HALF, 128), bf16),
            pltpu.VMEM((F, 2 * HALO, 128), bf16),
            pltpu.VMEM((F, 2 * HALO, 128), bf16),
            pltpu.VMEM((F, 2, SIDE, 128), bf16),
            pltpu.VMEM((F, 2, WIDTH, 128), f32),
            pltpu.VMEM((F, 256, 128), f32),
            dma((9,)), dma((F,)),
            dma((6,)), dma((6,)),
            dma((2, 5)), dma((2, 5)),
            dma((7,)), dma((7,)),
            dma((3,)), dma((3,)),
        ],
        compiler_params=pltpu.CompilerParams(
            collective_id=0, has_side_effects=True, vmem_limit_bytes=60 * 1024 * 1024
        ),
        name="adjoint_window",
    )(forcing, zonal_courant, meridional_courant, zonal_faces, meridional_faces, jnp.transpose(coupling, (1, 0, 2)))


def solution(mesh):
    return jax.shard_map(
        per_device,
        mesh=mesh,
        in_specs=(
            P("tm", None, None, None, "space"),
            P("tm", None, "space"),
            P("tm", None, "space"),
            P("tm", None, "space"),
            P("tm", None, "space"),
            P("tm", None, None),
        ),
        out_specs=P("tm", None, None, "space"),
        check_vma=False,
    )
```

```python
import jax
import jax.numpy as jnp
from jax import lax
from jax.experimental import pallas as pl
from jax.experimental.pallas import tpu as pltpu
from jax.sharding import PartitionSpec as P

OMEGA = 0.4
STEPS = 4
F = 6
WIDTH = 128
HALF = 64
HALO = 24
SIDE = 32
TS = (11, 14)
T = max(TS)
WEST = (12, 24)
ROWS = WIDTH + 2 * HALO
OPS = STEPS
EXT = ((0, 8, 8, 16, 16), (16, 16, 24, 24, 24))
MESH = pl.DeviceIdType.MESH
UNROLL = True


def body(
    forcing, courant_x, courant_y, faces_x, faces_y, coupling, out,
    nat_f, nat_o, even_odd, fr, op, cp, ops, ext_out, ext_in,
    co, mix, r, x1, x2, flux, r_n, x1_n, x2_n, adj, hand_out, hand_in, side_out, side_in, relay_in, res, outv,
    load_sem, out_sem, part_send, part_recv, ext_send, ext_recv,
    hand_send, hand_recv, res_send, res_recv,
):
    tm = lax.axis_index("tm")
    space = lax.axis_index("space")
    n_space = lax.axis_size("space")
    h = lax.rem(tm, 2)
    o = 1 - h
    pair = tm // 2

    def at_space(d):
        return lax.rem(space + d + n_space, n_space)

    ops_in = (faces_x, faces_y, courant_x, courant_y)
    loads = [pltpu.make_async_copy(ops_in[i].at[0], nat_o.at[i], load_sem.at[i]) for i in range(4)]
    loads.append(pltpu.make_async_copy(coupling, cp.at[h], load_sem.at[4]))
    loads += [pltpu.make_async_copy(forcing.at[0, k], nat_f.at[k], load_sem.at[5 + k]) for k in range(STEPS)]
    for i in (0, 1, 2, 3, 8):
        loads[i].start()

    barrier = pltpu.get_barrier_semaphore()
    count = 0
    for d in (-1, 1, 0):
        for j in range(4):
            if d == 0 and j == 0:
                continue
            other = lax.rem(tm + j, 4)
            pl.semaphore_signal(barrier, inc=1, device_id=(other, at_space(d)), device_id_type=MESH)
            count += 1

    partner = (2 * pair + o, space)
    to_east = (2 * pair, at_space(1))
    to_west = (2 * pair + 1, at_space(-1))

    def chunk(slot, c):
        return op.at[slot] if c == OPS else fr.at[slot, c]

    def partner_copy(c):
        ref = chunk(h, c).at[:, :, pl.ds(pl.multiple_of(HALO + 40 * o, 8), 88)]
        return pltpu.make_async_remote_copy(
            src_ref=ref, dst_ref=ref, send_sem=part_send.at[c], recv_sem=part_recv.at[c],
            device_id=partner, device_id_type=MESH,
        )

    def partner_arrival(c):
        ref = chunk(o, c).at[:, :, pl.ds(pl.multiple_of(HALO + 40 * h, 8), 88)]
        return pltpu.make_async_remote_copy(
            src_ref=ref, dst_ref=ref, send_sem=part_send.at[c], recv_sem=part_recv.at[c],
            device_id=partner, device_id_type=MESH,
        )

    def ext_pack(slot, c):
        n, ref = EXT[slot][c], chunk(slot, c)
        if n:
            for side in range(2):
                start = (HALO + WIDTH - n, HALO)[side]
                both = jnp.concatenate([ref[:, p, start:start + n] for p in range(2)], axis=1)
                ext_out[side, c, 0:both.shape[0], 0:2 * n] = both.astype(jnp.bfloat16)

    def ext_copies(slot, c):
        n, count = EXT[slot][c], chunk(slot, c).shape[0]
        if n == 0:
            return []
        return [
            pltpu.make_async_remote_copy(
                src_ref=ext_out.at[side, c, pl.ds(0, count), pl.ds(0, 2 * n)],
                dst_ref=ext_in.at[slot, c, pl.ds(0, count), pl.ds(0, 2 * n)],
                send_sem=ext_send.at[side, c], recv_sem=ext_recv.at[slot, c],
                device_id=(to_east, to_west)[side], device_id_type=MESH,
            )
            for side in range(2)
        ]

    def ext_start(slot, c):
        for copy in ext_copies(slot, c):
            copy.start()

    def ext_sent(slot, c):
        for copy in ext_copies(slot, c):
            copy.wait_send()

    def ext_arrival(slot, c):
        n, dest = EXT[slot][c], chunk(slot, c)
        ref = ext_in.at[slot, c, pl.ds(0, dest.shape[0]), pl.ds(0, 2 * n)]
        pltpu.make_async_remote_copy(
            src_ref=ref, dst_ref=ref, send_sem=ext_send.at[0, c], recv_sem=ext_recv.at[slot, c],
            device_id=to_east, device_id_type=MESH,
        ).wait_recv()
        start = pl.multiple_of((HALO - n) * o + (HALO + WIDTH) * h, 8)
        both = ext_in[slot, c, 0:dest.shape[0], 0:2 * n].astype(jnp.float32)
        for p in range(2):
            dest[:, p, pl.ds(start, n)] = both[:, p * n:(p + 1) * n]

    def wait_chunk(slot, c):
        @pl.when(h != slot)
        def _():
            partner_arrival(c).wait_recv()

        if EXT[slot][c]:
            ext_arrival(slot, c)

    def cp_copy(slot):
        return pltpu.make_async_remote_copy(
            src_ref=cp.at[slot], dst_ref=cp.at[slot],
            send_sem=part_send.at[5], recv_sem=part_recv.at[5],
            device_id=partner, device_id_type=MESH,
        )

    for slot in range(2):
        for c in range(STEPS + 1):
            n = EXT[slot][c]
            if n < HALO:
                ref = chunk(slot, c)
                start = pl.multiple_of((HALO + WIDTH + n) * h, 8)
                ref[:, :, pl.ds(start, HALO - n)] = jnp.zeros(ref.shape[:2] + (HALO - n, 128), jnp.float32)

    for i in range(4):
        loads[i].wait()
    for i in (4, 7, 6, 5):
        loads[i].start()
    for i in range(4):
        for p in range(2):
            op[h, i, p, HALO:HALO + WIDTH] = jnp.transpose(nat_o[i, pl.ds(p, 128, stride=2), :])
    def send_chunk(c):
        partner_copy(c).start()
        for slot in range(2):
            @pl.when(h == slot)
            def _(slot=slot):
                ext_pack(slot, c)
                if slot == 1:
                    ext_start(slot, c)

    early = lax.rem(space, 16) == 0

    @pl.when(jnp.logical_not(early))
    def _():
        pl.semaphore_wait(barrier, count)
        send_chunk(OPS)

    for k in (3, 2, 1, 0):
        loads[5 + k].wait()

        def one(f, carry, k=k):
            even_odd[...] = nat_f[k, f].astype(jnp.float32)
            for p in range(2):
                fr[h, k, f, p, HALO:HALO + WIDTH] = jnp.transpose(even_odd[pl.ds(p, 128, stride=2), :])
            return carry

        lax.fori_loop(0, F, one, 0)

        @pl.when(jnp.logical_not(early))
        def _(k=k):
            send_chunk(k)

    @pl.when(early)
    def _():
        pl.semaphore_wait(barrier, count)
        for c in (OPS, 3, 2, 1, 0):
            send_chunk(c)

    loads[4].wait()
    cp_copy(h).start()

    @pl.when(h == 0)
    def _():
        for c in (OPS, 3, 2, 1, 0):
            ext_start(0, c)

    lane = lax.broadcasted_iota(jnp.int32, (8, 128), 1)

    def frame(slot, t):
        return pl.ds(HALF * h + HALO - WEST[slot] + t, 8, stride=TS[slot])

    def coefficients(slot):
        @pl.when(h != slot)
        def _():
            cp_copy(o).wait_recv()

        last = TS[slot]
        for g in range(F):
            row = cp[slot, g]
            for f in range(F):
                value = jnp.broadcast_to(row[:, f:f + 1], (8, 128))
                mix[slot, g, f] = OMEGA * (value + 1.0) if g == f else OMEGA * value

        for p in range(2):
            for t in range(last):
                ops[t + 1, p] = op[slot, 0, p, frame(slot, t), :]
            ops[0, p] = pltpu.roll(ops[last, p], 1, 0)

        def one(t, carry):
            def get(i, p):
                return op[slot, i, p, frame(slot, t), :]

            b0, b1 = OMEGA * get(1, 0), OMEGA * get(1, 1)
            v0, v1 = 0.5 * OMEGA * get(3, 0), 0.5 * OMEGA * get(3, 1)
            north = (b0, jnp.where(lane == 127, 0.0, b1))
            south = (jnp.where(lane == 0, 0.0, pltpu.roll(b1, 1, 1)), b0)
            v_north = (v1, jnp.where(lane == 127, 0.0, pltpu.roll(v0, 127, 1)))
            v_south = (jnp.where(lane == 0, 0.0, -pltpu.roll(v1, 1, 1)), -v0)
            for p in range(2):
                east, west = OMEGA * ops[t + 1, p], OMEGA * ops[t, p]
                co[slot, t, p, 0] = (1.0 - OMEGA) - (east + west + north[p] + south[p])
                co[slot, t, p, 1] = east
                co[slot, t, p, 2] = west
                co[slot, t, p, 3] = (south, north)[p][p]
                co[slot, t, p, 4] = (north, south)[p][p]
                co[slot, t, p, 5] = 0.5 * OMEGA * get(2, p)
                co[slot, t, p, 6] = (v_south, v_north)[p][p]
                co[slot, t, p, 7] = (v_north, v_south)[p][p]
            return carry

        lax.fori_loop(0, last, one, 0)

    def pads(slot, buf):
        for p in range(2):
            buf[0, p] = pltpu.roll(buf[TS[slot], p], 1, 1)
            buf[TS[slot] + 1, p] = pltpu.roll(buf[1, p], 7, 1)

    def store(dst, dst_n, t, p, value):
        dst[t + 1, p] = value
        dst_n[t + 1, 1 - p] = pltpu.roll(value, 1 if p else 127, 2)

    def sweep(slot, src, src_n, dst, dst_n, add):
        def one(t, carry):
            for p in range(2):
                diag = co[slot, t, p, 0]
                if add is None:
                    value = (diag + 1.0) * src[t + 1, p]
                else:
                    value = diag * src[t + 1, p] + add[t + 1, p]
                value = value + co[slot, t, p, 1] * src[t + 2, p] + co[slot, t, p, 2] * src[t, p]
                value = value + co[slot, t, p, 3] * src_n[t + 1, p] + co[slot, t, p, 4] * src[t + 1, 1 - p]
                store(dst, dst_n, t, p, value)
                if add is not None:
                    flux[t + 1, p] = co[slot, t, p, 5] * value
            return carry

        lax.fori_loop(0, TS[slot], one, 0, unroll=UNROLL)
        pads(slot, dst if add is None else flux)

    def explicit_value(slot, k, t, p):
        value = fr[slot, k, :, p, frame(slot, t), :]
        value = value + flux[t + 2, p] - flux[t, p]
        value = value + co[slot, t, p, 6] * x2_n[t + 1, p] + co[slot, t, p, 7] * x2[t + 1, 1 - p]
        for g in range(F):
            value = value + mix[slot, g] * x2[t + 1, p, g]
        return value

    def step(slot, n):
        k = STEPS - 1 - n
        sweep(slot, r, r_n, x1, x1_n, None)
        sweep(slot, x1, x1_n, x2, x2_n, r)
        for c in range(STEPS):
            @pl.when((k == c) & (pair == 1))
            def _(c=c):
                wait_chunk(slot, c)

        return k

    def steps(slot, first):
        def one(n, carry):
            k = step(slot, n)

            def at(t, carry):
                for p in range(2):
                    store(r, r_n, t, p, explicit_value(slot, k, t, p))
                return carry

            lax.fori_loop(0, TS[slot], at, 0, unroll=UNROLL)
            pads(slot, r)
            return carry

        lax.fori_loop(first, STEPS - 1, one, 0)
        step(slot, STEPS - 1)
        for p in range(2):
            def at(t, carry, p=p):
                adj[1 - slot, :, p, adj_frame(slot, t), :] = explicit_value(slot, 0, t, p)
                return carry

            lax.fori_loop(0, TS[slot], at, 0, unroll=UNROLL)

            @pl.when(h == 1 - slot)
            def _(p=p):
                result_copy(1 - slot, p).start()

    def adj_frame(slot, t):
        return pl.ds(SIDE - WEST[slot] + t, 8, stride=TS[slot])

    def from_adj(slot):
        for t in range(TS[slot]):
            for p in range(2):
                store(r, r_n, t, p, adj[0, :, p, adj_frame(slot, t), :])
        pads(slot, r)

    def result_copy(phase, p):
        return pltpu.make_async_remote_copy(
            src_ref=adj.at[phase, :, p, pl.ds(SIDE, HALF)],
            dst_ref=res.at[:, p, pl.ds(pl.multiple_of(HALF * h, HALF), HALF)],
            send_sem=res_send.at[p], recv_sem=res_recv.at[p],
            device_id=partner, device_id_type=MESH,
        )

    def result_arrival(p):
        return pltpu.make_async_remote_copy(
            src_ref=adj.at[0, :, p, pl.ds(SIDE, HALF)],
            dst_ref=res.at[:, p, pl.ds(pl.multiple_of(HALF * o, HALF), HALF)],
            send_sem=res_send.at[p], recv_sem=res_recv.at[p],
            device_id=partner, device_id_type=MESH,
        )

    PIECES = [(inner, g) for inner in (True, False) for g in range(2)]

    def hand_main(n):
        inner, g = PIECES[n]
        ref = (pl.ds(F // 2 * g, F // 2), slice(None), pl.ds(pl.multiple_of(SIDE * (o if inner else h), SIDE), SIDE))
        return pltpu.make_async_remote_copy(
            src_ref=hand_out.at[ref], dst_ref=hand_in.at[ref], send_sem=hand_send.at[n], recv_sem=hand_recv.at[n],
            device_id=(h, space), device_id_type=MESH,
        )

    def hand_side():
        return pltpu.make_async_remote_copy(
            src_ref=side_out, dst_ref=side_in, send_sem=hand_send.at[4], recv_sem=hand_recv.at[4],
            device_id=(o, at_space(2 * h - 1)), device_id_type=MESH,
        )

    def relay(g):
        fields = pl.ds(F // 2 * g, F // 2)
        return pltpu.make_async_remote_copy(
            src_ref=hand_in.at[fields, :, pl.ds(pl.multiple_of(SIDE * o, SIDE), SIDE)], dst_ref=relay_in.at[fields],
            send_sem=hand_send.at[5 + g], recv_sem=hand_recv.at[5 + g],
            device_id=partner, device_id_type=MESH,
        )

    wait_chunk(1, OPS)
    coefficients(1)

    @pl.when(pair == 1)
    def _():
        wait_chunk(1, 3)
        for t in range(TS[1]):
            for p in range(2):
                store(r, r_n, t, p, fr[1, 3, :, p, frame(1, t), :])
        pads(1, r)

    @pl.when(pair == 0)
    def _():
        for c in range(STEPS):
            wait_chunk(1, c)
        wait_chunk(0, OPS)
        coefficients(0)
        for c in range(STEPS):
            wait_chunk(0, c)
        def take(fields, inner):
            rows = pl.multiple_of(SIDE * (o if inner else h), SIDE)
            adj[0, fields, :, pl.ds(SIDE + rows, SIDE)] = hand_in[fields, :, pl.ds(rows, SIDE)].astype(jnp.float32)

        for g in range(2):
            hand_main(g).wait_recv()
            relay(g).start()
            take(slice(F // 2 * g, F // 2 * (g + 1)), True)
        hand_side().wait_recv()
        both = side_in[...].astype(jnp.float32)
        for p in range(2):
            start = pl.multiple_of((SIDE - HALO) * o + (SIDE + HALF) * h, 8)
            adj[0, :, p, pl.ds(start, HALO)] = both[:, p * HALO:(p + 1) * HALO]
        for g in range(2):
            relay(g).wait_recv()
        adj[0, :, :, pl.ds(pl.multiple_of((SIDE + HALF) * o, SIDE), SIDE)] = relay_in[...].astype(jnp.float32)
        for g in range(2):
            hand_main(2 + g).wait_recv()
            take(slice(F // 2 * g, F // 2 * (g + 1)), False)
        from_adj(1)

    steps(1, pair)

    @pl.when(pair == 1)
    def _():
        wait_chunk(0, OPS)
        coefficients(0)

    from_adj(0)
    steps(0, 0)

    @pl.when(pair == 1)
    def _():
        start = pl.multiple_of(SIDE + (HALF - HALO) * h, 8)
        both = jnp.concatenate([adj[1, :, p, pl.ds(start, HALO)] for p in range(2)], axis=1)
        side_out[...] = both.astype(jnp.bfloat16)
        hand_side().start()
        for g in range(2):
            fields = slice(F // 2 * g, F // 2 * (g + 1))
            hand_out[fields] = adj[1, fields, :, SIDE:SIDE + HALF].astype(jnp.bfloat16)
            hand_main(g).start()
        for g in range(2):
            hand_main(2 + g).start()

    def out_copy(f):
        return pltpu.make_async_copy(outv.at[f], out.at[0, f], out_sem.at[f])

    own = adj.at[1 - h]
    res[:, :, pl.ds(pl.multiple_of(HALF * h, HALF), HALF)] = own[:, :, SIDE:SIDE + HALF]
    result_arrival(0).wait_recv()
    for f in range(F):
        outv[f, pl.ds(0, 128, stride=2), :] = jnp.transpose(res[f, 0])
    result_arrival(1).wait_recv()
    for f in range(F):
        outv[f, pl.ds(1, 128, stride=2), :] = jnp.transpose(res[f, 1])
        out_copy(f).start()

    for c in range(STEPS + 1):
        partner_copy(c).wait_send()
    for slot, left in ((0, (OPS, 3, 2, 1)), (1, (OPS, 3, 2, 1, 0))):
        @pl.when(h == slot)
        def _(slot=slot, left=left):
            for c in left:
                ext_sent(slot, c)

    cp_copy(h).wait_send()
    for p in range(2):
        result_copy(0, p).wait_send()

    @pl.when(pair == 1)
    def _():
        hand_side().wait_send()
        for n in range(4):
            hand_main(n).wait_send()

    @pl.when(pair == 0)
    def _():
        for g in range(2):
            relay(g).wait_send()

    for f in range(F):
        out_copy(f).wait()


def per_device(forcing, zonal_courant, meridional_courant, zonal_faces, meridional_faces, coupling):
    f32, bf16 = jnp.float32, jnp.bfloat16
    dma = pltpu.SemaphoreType.DMA
    state = pltpu.VMEM((T + 2, 2, F, 8, 128), f32)
    beside = pltpu.VMEM((T + 1, 2, F, 8, 128), f32)
    return pl.pallas_call(
        body,
        out_shape=jax.ShapeDtypeStruct((1,) + forcing.shape[2:], f32),
        in_specs=[pl.BlockSpec(memory_space=pl.ANY)] * 6,
        out_specs=pl.BlockSpec(memory_space=pl.ANY),
        scratch_shapes=[
            pltpu.VMEM((STEPS, F, 256, 128), bf16),
            pltpu.VMEM((4, 256, 128), f32),
            pltpu.VMEM((256, 128), f32),
            pltpu.VMEM((2, STEPS, F, 2, ROWS, 128), f32),
            pltpu.VMEM((2, 4, 2, ROWS, 128), f32),
            pltpu.VMEM((2, F, 1, F), f32),
            pltpu.VMEM((T + 1, 2, 8, 128), f32),
            pltpu.VMEM((2, STEPS + 1, F, 2 * HALO, 128), bf16),
            pltpu.VMEM((2, STEPS + 1, F, 2 * HALO, 128), bf16),
            pltpu.VMEM((2, T, 2, 8, 8, 128), f32),
            pltpu.VMEM((2, F, F, 8, 128), f32),
            state, state, state, state, beside, beside, beside,
            pltpu.VMEM((2, F, 2, HALF + 2 * SIDE, 128), f32),
            pltpu.VMEM((F, 2, HALF, 128), bf16),
            pltpu.VMEM((F, 2, HALF, 128), bf16),
            pltpu.VMEM((F, 2 * HALO, 128), bf16),
            pltpu.VMEM((F, 2 * HALO, 128), bf16),
            pltpu.VMEM((F, 2, SIDE, 128), bf16),
            pltpu.VMEM((F, 2, WIDTH, 128), f32),
            pltpu.VMEM((F, 256, 128), f32),
            dma((9,)), dma((F,)),
            dma((6,)), dma((6,)),
            dma((2, 5)), dma((2, 5)),
            dma((7,)), dma((7,)),
            dma((2,)), dma((2,)),
        ],
        compiler_params=pltpu.CompilerParams(
            collective_id=0, has_side_effects=True, vmem_limit_bytes=60 * 1024 * 1024
        ),
        name="adjoint_window",
    )(forcing, zonal_courant, meridional_courant, zonal_faces, meridional_faces, jnp.transpose(coupling, (1, 0, 2)))


def solution(mesh):
    return jax.shard_map(
        per_device,
        mesh=mesh,
        in_specs=(
            P("tm", None, None, None, "space"),
            P("tm", None, "space"),
            P("tm", None, "space"),
            P("tm", None, "space"),
            P("tm", None, "space"),
            P("tm", None, None),
        ),
        out_specs=P("tm", None, None, "space"),
        check_vma=False,
    )
```
